32 devices in a mesh: node: 4 (over y, core), edge: 8 (over z, x).
Axes of the slice: x: 2, y: 2, z: 4, core: 2. Of those that a mesh axis runs over, the one named last changes fastest.
Arguments:
- atoms: bfloat16 [4096, 1152], P(('node', 'edge')), may hold values from -6 to 6
- cotangent: bfloat16 [4096, 1152], P(('node', 'edge')), may hold values from -6 to 6
- params: float32 [409600], P('node'), may hold values from -4 to 4
- adam_m: float32 [409600], P('node'), may hold values from -4 to 4
- adam_v: float32 [409600], P('node'), may hold values from 0.3 to 3
- sends: int32 [4, 8, 128], P('node', 'edge'), may hold values from 0 to 127
- edge_slot: int32 [4096, 4], P(('node', 'edge')), may hold values from 0 to 127
- rot_index: int32 [4096, 4], P(('node', 'edge')), may hold values from 0 to 63
- rot_table: float32 [64, 9, 9], replicated, may hold values from -1.2 to 2, as said below
- edge_gain: float32 [4096, 4], P(('node', 'edge')), may hold values from 0.3 to 3
- live_tiles: int32 [4, 8], P('node', 'edge'), may hold values from 1 to 4, as said below
Outputs:
- output: bfloat16 [4096, 1152], P(('node', 'edge'))
- grad_atoms: bfloat16 [4096, 1152], P(('node', 'edge'))
- new_params: float32 [409600], P('node')
- new_moment_one: float32 [409600], P('node')
- new_moment_two: float32 [409600], P('node')
The draws below stay inside these ranges and needn't reach their ends.
Inputs may be any that keep to these rules, and one draw needn't show every extreme that they name: The first live_tiles[n, e] edge tiles of a device are live; some device has all 4 tiles live. `rot_table`: rotations of degrees 0, 1 and 2 act on harmonics 0, 1 to 3 and 4 to 8 only.
All inputs are finite; a program needn't handle non-finite values.
Results may differ from the reference program's by a relative error of at most 0.0015.
The reference program's roundings to bfloat16 on the way (of `weights`, `rotated`, `normed_low`, `hidden_low` and `grad_mixed`) count: a program that leaves them out, or rounds other values in their place, can miss the bound.
Values may be sent and summed in bfloat16 or wider, within the bound.
No kernel may reach another device: no remote copies, remote signals or barrier semaphores. Data moves between devices by JAX's collectives and lax.ppermute only.
A program may use at most 64 MiB of HBM per device.

```python
import math
import jax
import jax.numpy as jnp
import numpy as np
from jax import lax

C = 128
HARM = 9
FFH = 256
K = 4
TILE_ATOMS = 32
ROTS = 64
ATOM_DEV = 128
SLOTS = 16
TILES = 4
ATOMS = 4096
F = 1152
PARAMS = 409600
N_NODE = 4
N_EDGE = 8


harmonic_degree = np.array([0, 1, 1, 1, 2, 2, 2, 2, 2])


def draw_rot_table(key, part):
    noise_key = jax.random.fold_in(key, 11)
    noise_values = jax.random.truncated_normal(noise_key, -3.0, 3.0, (ROTS, 9, 9), jnp.float32)
    same_block = (harmonic_degree[:, None] == harmonic_degree[None, :]).astype(np.float32)
    block_scale = same_block / np.sqrt(2.0 * harmonic_degree + 1.0)[:, None]
    scaled = 0.4 * noise_values * jnp.asarray(block_scale, dtype=jnp.float32)
    return scaled + 0.8 * jnp.eye(9, dtype=jnp.float32)


def draw_live_tiles(key, part):
    count_key = jax.random.fold_in(key, 21)
    pick_key = jax.random.fold_in(key, 22)
    counts = jax.random.randint(count_key, (N_NODE * N_EDGE,), 1, TILES + 1)
    chosen = jax.random.randint(pick_key, (), 0, N_NODE * N_EDGE)
    filled = jnp.where(jnp.arange(N_NODE * N_EDGE) == chosen, TILES, counts)
    return filled.reshape(N_NODE, N_EDGE).astype(jnp.int32)


def touch_ends(values, rng, smallest, high):
    shape = values.shape
    spot = [jax.random.randint(jax.random.fold_in(rng, axis), (), 0, shape[axis]) for axis in range(len(shape))]
    values = values.at[tuple(spot)].set(smallest)
    longest = shape.index(max(shape))
    spot[longest] = (spot[longest] + 1) % shape[longest]
    return values.at[tuple(spot)].set(high)


def steps_of(stream_key, shape, cuts, least, high):
    loudness, own = 1.0, jax.random.fold_in(stream_key, 6)
    for axis_at, parts in cuts:
        draws = jnp.exp(jax.random.uniform(jax.random.fold_in(own, axis_at), (parts,), jnp.float32, least / len(cuts), high / len(cuts)))
        loudness = loudness * jnp.repeat(draws, shape[axis_at] // parts).reshape([-1 if axis == axis_at else 1 for axis in range(len(shape))])
    return loudness


def scatter_about(rng, shape, width, bound, shards=(), kind=jnp.bfloat16):
    drawn = jax.random.normal(rng, shape, jnp.float32) * width
    if len(shards) > 0:
        drawn = steps_of(rng, shape, shards, -0.22, 0.18) * drawn
    return jnp.clip(drawn, min=-bound, max=bound).astype(kind)


def setup_inputs(seed: int = 0) -> dict:
    key_of = jax.random.split(jax.random.key(seed), 12)
    return {
        "atoms": scatter_about(key_of[0], (ATOMS, F), 1.0, 6.0, ((0, 32),)),
        "cotangent": scatter_about(key_of[1], (ATOMS, F), 1.0, 6.0, ((0, 32),)),
        "params": scatter_about(key_of[2], (PARAMS,), 1.0, 4.0, ((0, 4),), jnp.float32),
        "adam_m": scatter_about(key_of[3], (PARAMS,), 1.0, 4.0, ((0, 4),), jnp.float32),
        "adam_v": jnp.clip(jnp.exp(math.log(3.0) - 2.3025851 * jax.random.uniform(key_of[4], (PARAMS,), jnp.float32) ** steps_of(key_of[4], (PARAMS,), ((0, 4),), -0.2, 0.2)), 0.3, 3.0),
        "sends": touch_ends(jax.random.randint(key_of[5], (N_NODE, N_EDGE, N_EDGE * SLOTS), 0, ATOM_DEV), jax.random.fold_in(key_of[5], 1), 0, ATOM_DEV - 1).astype(jnp.int32),
        "edge_slot": touch_ends(jax.random.randint(key_of[6], (ATOMS, K), 0, N_EDGE * SLOTS), jax.random.fold_in(key_of[6], 1), 0, (N_EDGE * SLOTS) - 1).astype(jnp.int32),
        "rot_index": touch_ends(jax.random.randint(key_of[7], (ATOMS, K), 0, ROTS), jax.random.fold_in(key_of[7], 1), 0, ROTS - 1).astype(jnp.int32),
        "rot_table": draw_rot_table(jax.random.fold_in(key_of[11], 71), 0),
        "edge_gain": jnp.clip(jnp.exp(math.log(3.0) - 2.3025851 * jax.random.uniform(key_of[9], (ATOMS, K), jnp.float32) ** steps_of(key_of[9], (ATOMS, K), ((0, 32),), -0.2, 0.2)), 0.3, 3.0),
        "live_tiles": draw_live_tiles(jax.random.fold_in(key_of[11], 71), 0),
    }


harmonic_order = (0, 2, 6, 3, 7, 1, 5, 8, 4)
highest = lax.Precision.HIGHEST
norm_epsilon = 1e-06
first_beta = 0.8
second_beta = 0.95
step_count = 100
learn_rate = 0.01
decay_rate = 0.01
adam_epsilon = 1e-08
grad_boost = 4.0

def unpack_weights(weights):
    lengths = [9 * C * C, 4 * C * C, 4 * C * C, C * C, C * C, C * FFH, C * FFH, FFH * C]
    starts = [0]
    for length in lengths:
        starts.append(starts[-1] + length)

    def take_piece(number, shape_pair):
        return weights[starts[number]:starts[number + 1]].reshape(shape_pair)
    zero_weight = take_piece(0, (3 * C, 3 * C))
    one_real = take_piece(1, (2 * C, 2 * C))
    one_imag = take_piece(2, (2 * C, 2 * C))
    two_real = take_piece(3, (C, C))
    two_imag = take_piece(4, (C, C))
    gate_weight = take_piece(5, (C, FFH))
    up_weight = take_piece(6, (C, FFH))
    down_weight = take_piece(7, (FFH, C))
    one_block = jnp.concatenate([jnp.concatenate([one_real, one_imag], axis=1), jnp.concatenate([-one_imag, one_real], axis=1)], axis=0)
    two_block = jnp.concatenate([jnp.concatenate([two_real, two_imag], axis=1), jnp.concatenate([-two_imag, two_real], axis=1)], axis=0)
    return (zero_weight, one_block, two_block, gate_weight, up_weight, down_weight)

def edge_forward(sources, rotation, edge_gains, matrices):
    zero_weight, one_block, two_block = (matrices[0], matrices[1], matrices[2])
    total_edges = sources.shape[0]
    rotated = jnp.einsum('eij,ejc->eic', rotation, sources.astype(jnp.float32), precision=highest).astype(jnp.bfloat16)
    zero_part = jnp.dot(rotated[:, 0:3].reshape(total_edges, 3 * C), zero_weight, preferred_element_type=jnp.float32) * (3 * C) ** (-0.5)
    one_part = jnp.dot(rotated[:, 3:7].reshape(total_edges, 4 * C), one_block, preferred_element_type=jnp.float32) * (4 * C) ** (-0.5)
    two_part = jnp.dot(rotated[:, 7:9].reshape(total_edges, 2 * C), two_block, preferred_element_type=jnp.float32) * (2 * C) ** (-0.5)
    mixed = jnp.concatenate([zero_part, one_part, two_part], axis=1).reshape(total_edges, HARM, C) * edge_gains[:, None, None]
    messages = jnp.einsum('eji,ejc->eic', rotation, mixed, precision=highest)
    return (rotated, messages)

def edge_backward(rotated, rotation, edge_gains, upstream, matrices):
    zero_weight, one_block, two_block = (matrices[0], matrices[1], matrices[2])
    total_edges = rotated.shape[0]
    grad_mixed = (jnp.einsum('eij,ejc->eic', rotation, upstream, precision=highest) * edge_gains[:, None, None]).astype(jnp.bfloat16)
    zero_in = rotated[:, 0:3].reshape(total_edges, 3 * C)
    one_in = rotated[:, 3:7].reshape(total_edges, 4 * C)
    two_in = rotated[:, 7:9].reshape(total_edges, 2 * C)
    zero_out = grad_mixed[:, 0:3].reshape(total_edges, 3 * C)
    one_out = grad_mixed[:, 3:7].reshape(total_edges, 4 * C)
    two_out = grad_mixed[:, 7:9].reshape(total_edges, 2 * C)
    zero_grad = jnp.dot(zero_in.T, zero_out, preferred_element_type=jnp.float32) * (3 * C) ** (-0.5)
    one_grad = jnp.dot(one_in.T, one_out, preferred_element_type=jnp.float32) * (4 * C) ** (-0.5)
    two_grad = jnp.dot(two_in.T, two_out, preferred_element_type=jnp.float32) * (2 * C) ** (-0.5)
    back_zero = jnp.dot(zero_out, zero_weight.T, preferred_element_type=jnp.float32) * (3 * C) ** (-0.5)
    back_one = jnp.dot(one_out, one_block.T, preferred_element_type=jnp.float32) * (4 * C) ** (-0.5)
    back_two = jnp.dot(two_out, two_block.T, preferred_element_type=jnp.float32) * (2 * C) ** (-0.5)
    grad_rotated = jnp.concatenate([back_zero, back_one, back_two], axis=1).reshape(total_edges, HARM, C)
    grad_sources = jnp.einsum('eij,eic->ejc', rotation, grad_rotated, precision=highest)
    return (grad_sources, (zero_grad, one_grad, two_grad))

def ffn_forward(atoms_block, aggregate, matrices):
    gate_weight, up_weight, down_weight = (matrices[3], matrices[4], matrices[5])
    number = atoms_block.shape[0]
    height = atoms_block.astype(jnp.float32).reshape(number, HARM, C) + aggregate
    inverse = lax.rsqrt(lax.optimization_barrier(jnp.mean(height * height, axis=(1, 2), keepdims=True)) + norm_epsilon)
    normed = height * inverse
    normed_low = normed.astype(jnp.bfloat16)
    gate_value = jax.nn.sigmoid(jnp.dot(normed_low[:, 0, :], gate_weight, preferred_element_type=jnp.float32) * C ** (-0.5))
    up_value = jnp.dot(normed_low.reshape(number * HARM, C), up_weight, preferred_element_type=jnp.float32).reshape(number, HARM, FFH) * C ** (-0.5)
    hidden_low = (up_value * gate_value[:, None, :]).astype(jnp.bfloat16)
    projected = jnp.dot(hidden_low.reshape(number * HARM, FFH), down_weight, preferred_element_type=jnp.float32).reshape(number, HARM, C)
    output = (height + projected * FFH ** (-0.5)).astype(jnp.bfloat16)
    return (output, (inverse, normed, normed_low, gate_value, up_value, hidden_low))

def ffn_backward(stored, cotangent, matrices):
    gate_weight, up_weight, down_weight = (matrices[3], matrices[4], matrices[5])
    inverse, normed, normed_low, gate_value, up_value, hidden_low = stored
    number = cotangent.shape[0]
    upstream = cotangent.reshape(number * HARM, C)
    down_grad = jnp.dot(hidden_low.reshape(number * HARM, FFH).T, upstream, preferred_element_type=jnp.float32) * FFH ** (-0.5)
    grad_hidden = jnp.dot(upstream, down_weight.T, preferred_element_type=jnp.float32).reshape(number, HARM, FFH) * FFH ** (-0.5)
    grad_up = (grad_hidden * gate_value[:, None, :]).astype(jnp.bfloat16)
    grad_gate = (lax.optimization_barrier(jnp.sum(grad_hidden * up_value, axis=1)) * gate_value * (1.0 - gate_value)).astype(jnp.bfloat16)
    up_grad = jnp.dot(normed_low.reshape(number * HARM, C).T, grad_up.reshape(number * HARM, FFH), preferred_element_type=jnp.float32) * C ** (-0.5)
    gate_grad = jnp.dot(normed_low[:, 0, :].T, grad_gate, preferred_element_type=jnp.float32) * C ** (-0.5)
    grad_normed = jnp.dot(grad_up.reshape(number * HARM, FFH), up_weight.T, preferred_element_type=jnp.float32).reshape(number, HARM, C) * C ** (-0.5)
    grad_normed = grad_normed.at[:, 0, :].add(jnp.dot(grad_gate, gate_weight.T, preferred_element_type=jnp.float32) * C ** (-0.5))
    grad_height = cotangent.astype(jnp.float32).reshape(number, HARM, C) + inverse * (grad_normed - normed * lax.optimization_barrier(jnp.mean(grad_normed * normed, axis=(1, 2), keepdims=True)))
    return (grad_height, (gate_grad, up_grad, down_grad))

def flat_grads(zero_grad, one_grad, two_grad, gate_grad, up_grad, down_grad):
    half_one = 2 * C
    one_real = one_grad[:half_one, :half_one] + one_grad[half_one:, half_one:]
    one_imag = one_grad[:half_one, half_one:] - one_grad[half_one:, :half_one]
    two_real = two_grad[:C, :C] + two_grad[C:, C:]
    two_imag = two_grad[:C, C:] - two_grad[C:, :C]
    pieces = [zero_grad, one_real, one_imag, two_real, two_imag, gate_grad, up_grad, down_grad]
    return jnp.concatenate([matrix.reshape(-1) for matrix in pieces])

def adam_step(params, moment_one, moment_two, gradient):
    new_one = first_beta * moment_one + (1.0 - first_beta) * gradient
    new_two = second_beta * moment_two + (1.0 - second_beta) * gradient * gradient
    corrected = new_one / (1.0 - first_beta ** step_count) / (jnp.sqrt(new_two / (1.0 - second_beta ** step_count)) + adam_epsilon)
    return (params - learn_rate * (corrected + decay_rate * params), new_one, new_two)

def reference(atoms, cotangent, params, adam_m, adam_v, sends, edge_slot, rot_index, rot_table, edge_gain, live_tiles):
    matrices = unpack_weights(params.astype(jnp.bfloat16))
    rot_rows = rot_table[:, jnp.array(harmonic_order, dtype=jnp.int32), :]
    device_count = N_NODE * N_EDGE
    atom_ids = jnp.arange(ATOMS, dtype=jnp.int32)
    device = atom_ids // ATOM_DEV
    node_of = device // N_EDGE
    edge_of = device % N_EDGE
    peer_of = edge_slot // SLOTS
    slot_place = edge_slot % SLOTS
    sent_row = sends[node_of[:, None], peer_of, edge_of[:, None] * SLOTS + slot_place]
    source = ((node_of[:, None] * N_EDGE + peer_of) * ATOM_DEV + sent_row).astype(jnp.int32)
    position = (atom_ids % ATOM_DEV)[:, None] * K + jnp.arange(K, dtype=jnp.int32)[None, :]
    live_mask = (position // (TILE_ATOMS * K) < live_tiles.reshape(-1)[device][:, None]).astype(jnp.float32)
    gains_all = edge_gain * live_mask
    source_blocks = source.reshape(device_count, ATOM_DEV, K)
    index_blocks = rot_index.reshape(device_count, ATOM_DEV, K)
    gain_blocks = gains_all.reshape(device_count, ATOM_DEV, K)

    def forward_block(inputs):
        source_block, index_block, gain_block = inputs
        sources = atoms[source_block.reshape(-1)].reshape(ATOM_DEV * K, HARM, C)
        rotation = rot_rows[index_block.reshape(-1)]
        rotated, messages = edge_forward(sources, rotation, gain_block.reshape(-1), matrices)
        return messages.reshape(ATOM_DEV, K, HARM, C).sum(axis=1) * K ** (-0.5)
    aggregate = lax.map(forward_block, (source_blocks, index_blocks, gain_blocks)).reshape(ATOMS, HARM, C)
    output, stored = ffn_forward(atoms, aggregate, matrices)
    grad_height, ffn_grads = ffn_backward(stored, cotangent, matrices)

    def backward_block(loop_state, inputs):
        accumulated, zero_acc, one_acc, two_acc = loop_state
        source_block, index_block, gain_block, height_block = inputs
        sources = atoms[source_block.reshape(-1)].reshape(ATOM_DEV * K, HARM, C)
        rotation = rot_rows[index_block.reshape(-1)]
        rotated, messages = edge_forward(sources, rotation, gain_block.reshape(-1), matrices)
        upstream = jnp.broadcast_to(height_block[:, None], (ATOM_DEV, K, HARM, C)).reshape(ATOM_DEV * K, HARM, C) * K ** (-0.5)
        grad_sources, weight_parts = edge_backward(rotated, rotation, gain_block.reshape(-1), upstream, matrices)
        accumulated = accumulated.at[source_block.reshape(-1)].add(grad_sources.reshape(ATOM_DEV * K, HARM * C))
        return ((accumulated, zero_acc + weight_parts[0], one_acc + weight_parts[1], two_acc + weight_parts[2]), None)
    initial = (jnp.zeros((ATOMS, HARM * C), jnp.float32), jnp.zeros((3 * C, 3 * C), jnp.float32), jnp.zeros((4 * C, 4 * C), jnp.float32), jnp.zeros((2 * C, 2 * C), jnp.float32))
    final_state, unused = lax.scan(backward_block, initial, (source_blocks, index_blocks, gain_blocks, grad_height.reshape(device_count, ATOM_DEV, HARM, C)))
    accumulated, zero_grad, one_grad, two_grad = final_state
    grad_atoms = (grad_height.reshape(ATOMS, HARM * C) + accumulated).astype(jnp.bfloat16)
    gradient = flat_grads(zero_grad, one_grad, two_grad, ffn_grads[0], ffn_grads[1], ffn_grads[2]) * (grad_boost * ATOMS ** (-0.5))
    new_params, new_one, new_two = adam_step(params, adam_m, adam_v, gradient)
    return (output.reshape(ATOMS, HARM * C), grad_atoms, new_params, new_one, new_two)
```

```python
import functools

import jax
import jax.numpy as jnp
from jax import lax
from jax.experimental import pallas as pl
from jax.experimental.pallas import tpu as pltpu
from jax.sharding import PartitionSpec as P

C = 128
HARM = 9
FFH = 256
K = 4
TILE_ATOMS = 32
ROTS = 64
EDGE_ROWS = 16

harmonic_order = (0, 2, 6, 3, 7, 1, 5, 8, 4)
norm_epsilon = 1e-06
first_beta = 0.8
second_beta = 0.95
step_count = 100
learn_rate = 0.01
decay_rate = 0.01
adam_epsilon = 1e-08
grad_boost = 4.0

F32 = jnp.float32
BF16 = jnp.bfloat16

degree_block = (0, 1, 1, 1, 2, 2, 2, 2, 2)
entries = [
    (row, col, harmonic_order[row] * HARM + col)
    for row in range(HARM)
    for col in range(HARM)
    if degree_block[harmonic_order[row]] == degree_block[col]
]
place_of = {(row, col): place for place, (row, col, _) in enumerate(entries)}
cols_of = [[col for r, col, _ in entries if r == row] for row in range(HARM)]
rows_of = [[row for row, c, _ in entries if c == col] for col in range(HARM)]

ZERO, ONE, TWO = 3 * C, 4 * C, 2 * C
row_scale = [ZERO**-0.5] * 3 + [ONE**-0.5] * 4 + [TWO**-0.5] * 2
piece_rows = [9 * C, 4 * C, 4 * C, C, C, 2 * C, 2 * C, 2 * C]
piece_start = [sum(piece_rows[:i]) for i in range(len(piece_rows))]
PACK_ROWS = sum(piece_rows)


def lanes(number, width=C):
    return slice(number * width, (number + 1) * width)


def dot(left, right, left_dim=1, right_dim=0):
    return lax.dot_general(
        left, right, (((left_dim,), (right_dim,)), ((), ())), preferred_element_type=F32
    )


def split_parts(value, count):
    parts = []
    for _ in range(count):
        part = value.astype(BF16)
        parts.append(part)
        value = value - part.astype(F32)
    return parts


def as_low(mask):
    return jnp.where(mask, 1.0, 0.0).astype(BF16)


def pick_kernel(sends_ref, atoms_ref, rows_ref):
    shape = (atoms_ref.shape[0], sends_ref.shape[1])
    picks = as_low(lax.broadcasted_iota(jnp.int32, shape, 0) == sends_ref[...])
    rows_ref[...] = dot(picks, atoms_ref[...], 0, 0).astype(BF16)


def main_kernel(node_count, edge_parts, all_atoms, *refs):
    (
        live_ref,
        rows_ref,
        atoms_ref,
        cot_ref,
        slot_ref,
        index_ref,
        gain_ref,
        table_ref,
    ) = refs[:8]
    shard_refs = refs[8 : 8 + node_count]
    (
        output_ref,
        height_grad_ref,
        slot_grad_ref,
        grads_ref,
        packed,
        zero_w,
        one_w,
        two_w,
        gate_w,
        up_w,
        down_w,
        turn,
        gains,
        source,
        rotated,
        mixed,
        height,
        normed_low,
        up_value,
        hidden,
        cot_low,
        grad_up,
        grad_mixed,
    ) = refs[8 + node_count :]
    atoms_n = atoms_ref.shape[0]
    slots_n = rows_ref.shape[0]
    edges_n = atoms_n * K
    node = lax.axis_index("node")

    shard_rows = PACK_ROWS // node_count
    for distance in range(node_count):
        first = pl.multiple_of((node ^ distance) * shard_rows, 8)
        packed[pl.ds(first, shard_rows), :] = shard_refs[distance][...].astype(F32)

    def unpack(piece, rows, width):
        return [
            packed[pl.ds(piece_start[piece] + part, rows, stride=width), :].astype(BF16)
            for part in range(width)
        ]

    for part, block in enumerate(unpack(0, ZERO, 3)):
        zero_w[:, lanes(part)] = block
    for part, block in enumerate(unpack(1, 2 * C, 2)):
        one_w[0 : 2 * C, lanes(part)] = block
        one_w[2 * C : 4 * C, lanes(part + 2)] = block
    for part, block in enumerate(unpack(2, 2 * C, 2)):
        one_w[0 : 2 * C, lanes(part + 2)] = block
        one_w[2 * C : 4 * C, lanes(part)] = -block
    (block,) = unpack(3, C, 1)
    two_w[0:C, 0:C] = block
    two_w[C : 2 * C, C : 2 * C] = block
    (block,) = unpack(4, C, 1)
    two_w[0:C, C : 2 * C] = block
    two_w[C : 2 * C, 0:C] = -block
    for part, block in enumerate(unpack(5, C, 2)):
        gate_w[:, lanes(part)] = block
    for part, block in enumerate(unpack(6, C, 2)):
        up_w[:, lanes(part)] = block
    (block,) = unpack(7, FFH, 1)
    down_w[...] = block

    table = jnp.concatenate(split_parts(table_ref[...], 3), axis=0)
    table_range = lax.broadcasted_iota(jnp.int32, (atoms_n, ROTS), 1)
    slot_range = lax.broadcasted_iota(jnp.int32, (atoms_n, slots_n), 1)
    atom_range = lax.broadcasted_iota(jnp.int32, (atoms_n, C), 0)
    is_live = atom_range < live_ref[0, 0] * TILE_ATOMS
    for k in range(K):
        rows = slice(k * atoms_n, (k + 1) * atoms_n)
        chosen = as_low(index_ref[:, k : k + 1] == table_range)
        turns = dot(jnp.concatenate([chosen] * 3, axis=1), table)
        for place, (_, _, entry) in enumerate(entries):
            turn[place, rows, :] = jnp.broadcast_to(turns[:, entry : entry + 1], (atoms_n, C))
        gain = jnp.broadcast_to(gain_ref[:, k : k + 1], (atoms_n, C))
        gains[rows, :] = jnp.where(is_live, gain, 0.0) * K**-0.5
        taken = as_low(slot_ref[:, k : k + 1] == slot_range)
        source[rows, :] = dot(taken, rows_ref[...])

    def rotate(step, carry):
        rows = pl.ds(pl.multiple_of(step * EDGE_ROWS, EDGE_ROWS), EDGE_ROWS)
        values = [source[rows, lanes(col)] for col in range(HARM)]
        for row in range(HARM):
            total = sum(turn[place_of[row, col], rows, :] * values[col] for col in cols_of[row])
            rotated[rows, lanes(row)] = total.astype(BF16)
        return carry

    lax.fori_loop(0, edges_n // EDGE_ROWS, rotate, 0)
    mixed[:, 0:ZERO] = dot(rotated[:, 0:ZERO], zero_w[...])
    mixed[:, ZERO : ZERO + ONE] = dot(rotated[:, ZERO : ZERO + ONE], one_w[...])
    mixed[:, ZERO + ONE :] = dot(rotated[:, ZERO + ONE :], two_w[...])

    def atom_slice(step, base=0):
        return pl.ds(pl.multiple_of(base + step * EDGE_ROWS, EDGE_ROWS), EDGE_ROWS)

    def gather_messages(step, carry):
        here = atom_slice(step)
        totals = [atoms_ref[here, lanes(col)].astype(F32) for col in range(HARM)]
        for k in range(K):
            rows = atom_slice(step, k * atoms_n)
            gain = gains[rows, :]
            for row in range(HARM):
                value = mixed[rows, lanes(row)] * (gain * row_scale[row])
                for col in cols_of[row]:
                    totals[col] = totals[col] + turn[place_of[row, col], rows, :] * value
        squares = sum(total * total for total in totals)
        mean = jnp.sum(squares, axis=1, keepdims=True) * (1.0 / (HARM * C))
        inverse = lax.rsqrt(mean + norm_epsilon)
        for col in range(HARM):
            height[atom_slice(step, col * atoms_n), :] = totals[col]
            normed_low[atom_slice(step, col * atoms_n), :] = (totals[col] * inverse).astype(BF16)
            cot_low[atom_slice(step, col * atoms_n), :] = cot_ref[here, lanes(col)]
        return carry

    lax.fori_loop(0, atoms_n // EDGE_ROWS, gather_messages, 0)

    gate = jax.nn.sigmoid(dot(normed_low[0:atoms_n, :], gate_w[...]) * C**-0.5)
    up_value[...] = dot(normed_low[...], up_w[...]) * C**-0.5
    for col in range(HARM):
        rows = lanes(col, atoms_n)
        hidden[rows, :] = (up_value[rows, :] * gate).astype(BF16)
    projected = dot(hidden[...], down_w[...]) * FFH**-0.5
    for col in range(HARM):
        rows = lanes(col, atoms_n)
        output_ref[:, lanes(col)] = (height[rows, :] + projected[rows, :]).astype(BF16)
    grad_hidden = dot(cot_low[...], down_w[...], 1, 1) * FFH**-0.5
    gate_sum = jnp.zeros_like(gate)
    for col in range(HARM):
        rows = lanes(col, atoms_n)
        grad_up[rows, :] = (grad_hidden[rows, :] * gate).astype(BF16)
        gate_sum = gate_sum + grad_hidden[rows, :] * up_value[rows, :]
    grad_gate = (gate_sum * gate * (1.0 - gate)).astype(BF16)
    grad_normed = dot(grad_up[...], up_w[...], 1, 1) * C**-0.5
    gate_normed = dot(grad_gate, gate_w[...], 1, 1) * C**-0.5
    heights = [height[lanes(col, atoms_n), :] for col in range(HARM)]
    squares = sum(value * value for value in heights)
    mean = jnp.sum(squares, axis=1, keepdims=True) * (1.0 / (HARM * C))
    inverse = lax.rsqrt(mean + norm_epsilon)
    along = [grad_normed[lanes(col, atoms_n), :] for col in range(HARM)]
    along[0] = along[0] + gate_normed
    overlap = sum(along[col] * heights[col] for col in range(HARM)) * inverse
    overlap = jnp.sum(overlap, axis=1, keepdims=True) * (1.0 / (HARM * C))
    for col in range(HARM):
        rows = lanes(col, atoms_n)
        height_grad_ref[rows, :] = cot_low[rows, :].astype(F32) + inverse * (
            along[col] - heights[col] * (inverse * overlap)
        )

    def rotate_grads(step, carry):
        values = [height_grad_ref[atom_slice(step, col * atoms_n), :] for col in range(HARM)]
        for k in range(K):
            rows = atom_slice(step, k * atoms_n)
            gain = gains[rows, :]
            for row in range(HARM):
                total = sum(turn[place_of[row, col], rows, :] * values[col] for col in cols_of[row])
                grad_mixed[rows, lanes(row)] = (total * gain).astype(BF16)
        return carry

    lax.fori_loop(0, atoms_n // EDGE_ROWS, rotate_grads, 0)
    boost = grad_boost * all_atoms**-0.5

    def pack_piece(piece, rows, width, value):
        for part in range(width):
            packed[pl.ds(piece_start[piece] + part, rows, stride=width), :] = value[:, lanes(part)]

    zero_grad = dot(rotated[:, 0:ZERO], grad_mixed[:, 0:ZERO], 0, 0) * (row_scale[0] * boost)
    pack_piece(0, ZERO, 3, zero_grad)
    one_in = rotated[:, ZERO : ZERO + ONE]
    one_out = grad_mixed[:, ZERO : ZERO + ONE]
    one_grad = dot(one_in, one_out, 0, 0) * (row_scale[3] * boost)
    half = 2 * C
    pack_piece(1, half, 2, one_grad[:half, :half] + one_grad[half:, half:])
    pack_piece(2, half, 2, one_grad[:half, half:] - one_grad[half:, :half])
    two_grad = dot(rotated[:, ZERO + ONE :], grad_mixed[:, ZERO + ONE :], 0, 0)
    two_grad = two_grad * (row_scale[7] * boost)
    pack_piece(3, C, 1, two_grad[:C, :C] + two_grad[C:, C:])
    pack_piece(4, C, 1, two_grad[:C, C:] - two_grad[C:, :C])
    pack_piece(5, C, 2, dot(normed_low[0:atoms_n, :], grad_gate, 0, 0) * (C**-0.5 * boost))
    pack_piece(6, C, 2, dot(normed_low[...], grad_up[...], 0, 0) * (C**-0.5 * boost))
    pack_piece(7, FFH, 1, dot(hidden[...], cot_low[...], 0, 0) * (FFH**-0.5 * boost))
    part_rows = shard_rows // edge_parts
    edge_low = lax.axis_index("edge") & (edge_parts - 1)
    bits = node_count.bit_length() - 1
    for place in range(node_count):
        distance = int(format(place, "b").zfill(bits)[::-1], 2) if bits else 0
        for part in range(edge_parts):
            first = (node ^ distance) * shard_rows + (edge_low ^ part) * part_rows
            values = packed[pl.ds(pl.multiple_of(first, 8), part_rows), :]
            grads_ref[lanes(place * edge_parts + part, part_rows), :] = values.astype(BF16)

    mixed[:, 0:ZERO] = dot(grad_mixed[:, 0:ZERO], zero_w[...], 1, 1)
    mixed[:, ZERO : ZERO + ONE] = dot(grad_mixed[:, ZERO : ZERO + ONE], one_w[...], 1, 1)
    mixed[:, ZERO + ONE :] = dot(grad_mixed[:, ZERO + ONE :], two_w[...], 1, 1)

    def rotate_back(step, carry):
        rows = pl.ds(pl.multiple_of(step * EDGE_ROWS, EDGE_ROWS), EDGE_ROWS)
        values = [mixed[rows, lanes(row)] * row_scale[row] for row in range(HARM)]
        for col in range(HARM):
            source[rows, lanes(col)] = sum(
                turn[place_of[row, col], rows, :] * values[row] for row in rows_of[col]
            )
        return carry

    lax.fori_loop(0, edges_n // EDGE_ROWS, rotate_back, 0)
    parts = []
    for k in range(K):
        parts.append(as_low(slot_ref[:, k : k + 1] == slot_range))
    taken = jnp.concatenate(parts, axis=0)
    for col in range(HARM):
        pieces = split_parts(source[:, lanes(col)], 3)
        slot_grad_ref[:, lanes(col)] = sum(dot(taken, piece, 0, 0) for piece in pieces)


def finish_kernel(sends_ref, height_grad_ref, back_ref, grad_ref):
    atoms_n = grad_ref.shape[0]
    shape = (atoms_n, sends_ref.shape[1])
    picks = as_low(lax.broadcasted_iota(jnp.int32, shape, 0) == sends_ref[...])
    for col in range(HARM):
        pieces = split_parts(back_ref[:, lanes(col)], 3)
        total = sum(dot(picks, piece) for piece in pieces)
        grad_ref[:, lanes(col)] = (height_grad_ref[lanes(col, atoms_n), :] + total).astype(BF16)


def adam_step(params, moment_one, moment_two, gradient):
    new_one = first_beta * moment_one + (1.0 - first_beta) * gradient
    new_two = second_beta * moment_two + (1.0 - second_beta) * gradient * gradient
    corrected = (
        new_one
        / (1.0 - first_beta**step_count)
        / (jnp.sqrt(new_two / (1.0 - second_beta**step_count)) + adam_epsilon)
    )
    return (params - learn_rate * (corrected + decay_rate * params), new_one, new_two)


def swap(value, axis, bit):
    size = lax.axis_size(axis)
    return lax.ppermute(value, axis, [(i, i ^ (1 << bit)) for i in range(size)])


def shards(
    atoms,
    cotangent,
    params,
    adam_m,
    adam_v,
    sends,
    edge_slot,
    rot_index,
    rot_table,
    edge_gain,
    live_tiles,
):
    node_size = lax.axis_size("node")
    edge_size = lax.axis_size("edge")
    node_bits = node_size.bit_length() - 1
    edge_bits = edge_size.bit_length() - 1
    atoms_n, features = atoms.shape
    slots_n = sends.shape[-1]
    per_peer = slots_n // edge_size
    edges_n = atoms_n * K
    edge_parts = 2 if edge_bits else 1
    vmem = pl.BlockSpec(memory_space=pltpu.VMEM)
    smem = pl.BlockSpec(memory_space=pltpu.SMEM)

    own = params.reshape(-1, C).astype(BF16)
    shard_list = [own]
    by_distance = {0: own}
    for bit in reversed(range(node_bits)):
        for distance in list(by_distance):
            by_distance[distance | (1 << bit)] = swap(by_distance[distance], "node", bit)
    shard_list = [by_distance[distance] for distance in range(node_size)]

    send_rows = sends.reshape(1, slots_n)
    outgoing = pl.pallas_call(
        pick_kernel,
        out_shape=jax.ShapeDtypeStruct((slots_n, features), BF16),
        in_specs=[vmem] * 2,
        out_specs=vmem,
        name="pick",
    )(send_rows, atoms)
    slot_rows = lax.all_to_all(
        outgoing.reshape(edge_size, per_peer, features),
        "edge",
        split_axis=0,
        concat_axis=0,
        tiled=True,
    ).reshape(slots_n, features)

    f32_rows = functools.partial(pltpu.VMEM, dtype=F32)
    low_rows = functools.partial(pltpu.VMEM, dtype=BF16)
    output, height_grad, slot_grad, grads = pl.pallas_call(
        functools.partial(main_kernel, node_size, edge_parts, atoms_n * node_size * edge_size),
        out_shape=(
            jax.ShapeDtypeStruct((atoms_n, features), BF16),
            jax.ShapeDtypeStruct((HARM * atoms_n, C), F32),
            jax.ShapeDtypeStruct((slots_n, features), F32),
            jax.ShapeDtypeStruct((PACK_ROWS, C), BF16),
        ),
        in_specs=[smem] + [vmem] * (7 + node_size),
        out_specs=(vmem,) * 4,
        scratch_shapes=[
            pltpu.VMEM((PACK_ROWS, C), F32),
            pltpu.VMEM((ZERO, ZERO), BF16),
            pltpu.VMEM((ONE, ONE), BF16),
            pltpu.VMEM((TWO, TWO), BF16),
            pltpu.VMEM((C, FFH), BF16),
            pltpu.VMEM((C, FFH), BF16),
            pltpu.VMEM((FFH, C), BF16),
            pltpu.VMEM((len(entries), edges_n, C), F32),
            pltpu.VMEM((edges_n, C), F32),
            pltpu.VMEM((edges_n, features), F32),
            pltpu.VMEM((edges_n, features), BF16),
            pltpu.VMEM((edges_n, features), F32),
            pltpu.VMEM((HARM * atoms_n, C), F32),
            pltpu.VMEM((HARM * atoms_n, C), BF16),
            pltpu.VMEM((HARM * atoms_n, FFH), F32),
            pltpu.VMEM((HARM * atoms_n, FFH), BF16),
            pltpu.VMEM((HARM * atoms_n, C), BF16),
            pltpu.VMEM((HARM * atoms_n, FFH), BF16),
            pltpu.VMEM((edges_n, features), BF16),
        ],
        name="layer",
    )(
        live_tiles,
        slot_rows,
        atoms,
        cotangent,
        edge_slot,
        rot_index,
        edge_gain,
        rot_table.reshape(ROTS, HARM * HARM),
        *shard_list,
    )

    for bit in range(node_bits):
        half = grads.shape[0] // 2
        came = swap(grads[half:], "node", bit)
        grads = (grads[:half].astype(F32) + came.astype(F32)).astype(BF16)
    if edge_bits:
        half = grads.shape[0] // 2
        came = swap(grads[half:], "edge", 0)
        grads = (grads[:half].astype(F32) + came.astype(F32)).astype(BF16)
        for bit in range(1, edge_bits):
            came = swap(grads, "edge", bit)
            grads = (grads.astype(F32) + came.astype(F32)).astype(BF16)
        other = swap(grads, "edge", 0)
        is_low = (lax.axis_index("edge") & 1) == 0
        grads = jnp.concatenate(
            [jnp.where(is_low, grads, other), jnp.where(is_low, other, grads)], axis=0
        )

    returned = lax.all_to_all(
        slot_grad.reshape(edge_size, per_peer, features),
        "edge",
        split_axis=0,
        concat_axis=0,
        tiled=True,
    ).reshape(slots_n, features)
    grad_atoms = pl.pallas_call(
        finish_kernel,
        out_shape=jax.ShapeDtypeStruct((atoms_n, features), BF16),
        in_specs=[vmem] * 3,
        out_specs=vmem,
        name="finish",
    )(send_rows, height_grad, returned)

    def rows_of_lanes(value):
        return value.reshape(-1, C)

    new_params, new_one, new_two = adam_step(
        rows_of_lanes(params), rows_of_lanes(adam_m), rows_of_lanes(adam_v), grads.astype(F32)
    )
    return (
        output,
        grad_atoms,
        new_params.reshape(-1),
        new_one.reshape(-1),
        new_two.reshape(-1),
    )


def solution(mesh):
    return jax.shard_map(
        shards,
        mesh=mesh,
        in_specs=(
            P(("node", "edge"), None),
            P(("node", "edge"), None),
            P("node"),
            P("node"),
            P("node"),
            P("node", "edge", None),
            P(("node", "edge"), None),
            P(("node", "edge"), None),
            P(),
            P(("node", "edge"), None),
            P("node", "edge"),
        ),
        out_specs=(
            P(("node", "edge"), None),
            P(("node", "edge"), None),
            P("node"),
            P("node"),
            P("node"),
        ),
        check_vma=False,
    )
```

```python
import functools

import jax
import jax.numpy as jnp
from jax import lax
from jax.experimental import pallas as pl
from jax.experimental.pallas import tpu as pltpu
from jax.sharding import PartitionSpec as P

C = 128
HARM = 9
FFH = 256
K = 4
TILE_ATOMS = 32
ROTS = 64
SUB = 8
TURN_ROWS = 88

harmonic_order = (0, 2, 6, 3, 7, 1, 5, 8, 4)
norm_epsilon = 1e-06
first_beta = 0.8
second_beta = 0.95
step_count = 100
learn_rate = 0.01
decay_rate = 0.01
adam_epsilon = 1e-08
grad_boost = 4.0

F32 = jnp.float32
BF16 = jnp.bfloat16

degree_block = (0, 1, 1, 1, 2, 2, 2, 2, 2)
entries = [
    (row, col, harmonic_order[row] * HARM + col)
    for row in range(HARM)
    for col in range(HARM)
    if degree_block[harmonic_order[row]] == degree_block[col]
]
place_of = {(row, col): place for place, (row, col, _) in enumerate(entries)}
cols_of = [[col for r, col, _ in entries if r == row] for row in range(HARM)]
rows_of = [[row for row, c, _ in entries if c == col] for col in range(HARM)]

ZERO, ONE, TWO = 3 * C, 4 * C, 2 * C
row_scale = [ZERO**-0.5] * 3 + [ONE**-0.5] * 4 + [TWO**-0.5] * 2
piece_rows = [9 * C, 4 * C, 4 * C, C, C, 2 * C, 2 * C, 2 * C]
piece_start = [sum(piece_rows[:i]) for i in range(len(piece_rows))]
PACK_ROWS = sum(piece_rows)


def lanes(number, width=C):
    return slice(number * width, (number + 1) * width)


def dot(left, right, left_dim=1, right_dim=0):
    return lax.dot_general(
        left, right, (((left_dim,), (right_dim,)), ((), ())), preferred_element_type=F32
    )


def split_parts(value, count):
    parts = []
    for _ in range(count):
        part = value.astype(BF16)
        parts.append(part)
        value = value - part.astype(F32)
    return parts


def as_low(mask):
    return jnp.where(mask, 1.0, 0.0).astype(BF16)


def pick_kernel(sends_ref, atoms_ref, rows_ref):
    shape = (atoms_ref.shape[0], sends_ref.shape[1])
    picks = as_low(lax.broadcasted_iota(jnp.int32, shape, 0) == sends_ref[...])
    rows_ref[...] = dot(picks, atoms_ref[...], 0, 0).astype(BF16)


def prepare_kernel(node_count, *refs):
    atoms_ref, cot_ref, index_ref, table_ref = refs[:4]
    shard_refs = refs[4 : 4 + node_count]
    (
        zero_ref,
        one_ref,
        two_ref,
        zero_t_ref,
        one_t_ref,
        two_t_ref,
        gate_ref,
        up_ref,
        down_ref,
        gate_t_ref,
        up_t_ref,
        down_t_ref,
        atoms_t_ref,
        cot_t_ref,
        turn_ref,
        packed,
    ) = refs[4 + node_count :]
    atoms_n = atoms_ref.shape[0]
    node = lax.axis_index("node")

    shard_rows = PACK_ROWS // node_count
    for distance in range(node_count):
        first = pl.multiple_of((node ^ distance) * shard_rows, 8)
        packed[pl.ds(first, shard_rows), :] = shard_refs[distance][...].astype(F32)

    def unpack(piece, rows, width, *targets):
        for part in range(width):
            first = piece_start[piece] + part
            block = packed[pl.ds(first, rows, stride=width), :].astype(BF16)
            for target, turned, row, col, sign in targets:
                value = block if sign > 0 else -block
                if turned:
                    target[col + part * C : col + (part + 1) * C, row : row + rows] = value.T
                else:
                    target[row : row + rows, col + part * C : col + (part + 1) * C] = value

    half = 2 * C
    unpack(0, ZERO, 3, (zero_ref, False, 0, 0, 1), (zero_t_ref, True, 0, 0, 1))
    for piece, (matrix, turned, rows) in (
        (1, (one_ref, one_t_ref, half)),
        (3, (two_ref, two_t_ref, C)),
    ):
        width = rows // C
        unpack(
            piece,
            rows,
            width,
            (matrix, False, 0, 0, 1),
            (matrix, False, rows, rows, 1),
            (turned, True, 0, 0, 1),
            (turned, True, rows, rows, 1),
        )
        unpack(
            piece + 1,
            rows,
            width,
            (matrix, False, 0, rows, 1),
            (matrix, False, rows, 0, -1),
            (turned, True, 0, rows, 1),
            (turned, True, rows, 0, -1),
        )
    unpack(5, C, 2, (gate_ref, False, 0, 0, 1), (gate_t_ref, True, 0, 0, 1))
    unpack(6, C, 2, (up_ref, False, 0, 0, 1), (up_t_ref, True, 0, 0, 1))
    unpack(7, FFH, 1, (down_ref, False, 0, 0, 1), (down_t_ref, True, 0, 0, 1))

    for col in range(HARM):
        atoms_t_ref[:, lanes(col, atoms_n)] = atoms_ref[:, lanes(col)].T
        cot_t_ref[:, lanes(col, atoms_n)] = cot_ref[:, lanes(col)].T
    pieces = split_parts(table_ref[...], 3)
    range_of_table = lax.broadcasted_iota(jnp.int32, (ROTS, atoms_n), 0)
    for k in range(K):
        chosen = as_low(range_of_table == index_ref[k : k + 1, :])
        turn_ref[pl.ds(k * TURN_ROWS, HARM * HARM), :] = sum(dot(piece, chosen) for piece in pieces)


def turns_of(turn_ref, k, factors=None):
    values = {}
    for row, col, entry in entries:
        value = turn_ref[pl.ds(k * TURN_ROWS + entry, SUB, stride=0), :]
        values[row, col] = value if factors is None else value * factors[row]
    return values


def over_channels(body):
    def step(number, carry):
        body(pl.multiple_of(number * 2 * SUB, 2 * SUB))
        return carry

    lax.fori_loop(0, C // (2 * SUB), step, 0)


def rows_at(harmonic, first, count=SUB):
    return pl.ds(pl.multiple_of(harmonic * C + first, SUB), count)


def main_kernel(edge_parts, node_count, all_atoms, *refs):
    (
        live_ref,
        rows_ref,
        slot_ref,
        gain_ref,
        zero_t,
        one_t,
        two_t,
        gate_w,
        up_w,
        down_w,
        gate_t,
        up_t,
        down_t,
        atoms_t,
        cot_t,
        turn,
        output_ref,
        height_grad,
        grad_mixed,
        keep_ref,
        send_ref,
        source,
        rotated,
        mixed,
        height,
        normed_low,
        up_value,
        hidden,
        grad_up,
        packed,
    ) = refs
    atoms_n = output_ref.shape[0]
    slots_n = rows_ref.shape[0]
    node = lax.axis_index("node")

    slot_range = lax.broadcasted_iota(jnp.int32, (slots_n, atoms_n), 0)
    for k in range(K):
        taken = as_low(slot_range == slot_ref[k : k + 1, :])
        source[:, lanes(k, atoms_n)] = dot(rows_ref[...], taken, 0, 0)
    is_live = lax.broadcasted_iota(jnp.int32, (1, atoms_n), 1) < live_ref[0, 0] * TILE_ATOMS
    gains = jnp.where(is_live, gain_ref[...], 0.0) * K**-0.5

    for k in range(K):
        here = lanes(k, atoms_n)
        turns = turns_of(turn, k)

        def rotate(first, here=here, turns=turns):
            halves = []
            for start in (0, SUB):
                values = [source[rows_at(col, first + start), here] for col in range(HARM)]
                halves.append(
                    [
                        sum(turns[row, col] * values[col] for col in cols_of[row])
                        for row in range(HARM)
                    ]
                )
            for row in range(HARM):
                pair = jnp.concatenate([halves[0][row], halves[1][row]], axis=0)
                rotated[rows_at(row, first, 2 * SUB), here] = pair.astype(BF16)

        over_channels(rotate)
    one_rows = slice(ZERO, ZERO + ONE)
    two_rows = slice(ZERO + ONE, HARM * C)
    mixed[0:ZERO, :] = dot(zero_t[...], rotated[0:ZERO, :])
    mixed[one_rows, :] = dot(one_t[...], rotated[one_rows, :])
    mixed[two_rows, :] = dot(two_t[...], rotated[two_rows, :])

    for k in range(K):
        here = lanes(k, atoms_n)
        gain = jnp.broadcast_to(gains[k : k + 1, :], (SUB, atoms_n))
        turns = turns_of(turn, k, [gain * scale for scale in row_scale])

        def gather_messages(first, k=k, here=here, turns=turns):
            if k == 0:
                starts = [
                    atoms_t[pl.ds(first, 2 * SUB), lanes(col, atoms_n)].astype(F32)
                    for col in range(HARM)
                ]
            for start in (0, SUB):
                values = [mixed[rows_at(row, first + start), here] for row in range(HARM)]
                target = pl.ds(pl.multiple_of(first + start, SUB), SUB)
                for col in range(HARM):
                    there = lanes(col, atoms_n)
                    base = starts[col][start : start + SUB] if k == 0 else height[target, there]
                    total = sum(turns[row, col] * values[row] for row in rows_of[col])
                    height[target, there] = base + total

        over_channels(gather_messages)

    def atom_sum(value):
        total = sum(value[:, lanes(col, atoms_n)] for col in range(HARM))
        return jnp.sum(total, axis=0, keepdims=True)

    def each(value):
        return jnp.concatenate([value] * HARM, axis=1)

    mean = atom_sum(height[...] * height[...]) * (1.0 / (HARM * C))
    inverse = lax.rsqrt(mean + norm_epsilon)
    normed_low[...] = (height[...] * each(inverse)).astype(BF16)
    gate = jax.nn.sigmoid(dot(gate_t[...], normed_low[:, 0:atoms_n]) * C**-0.5)
    gate_each = each(gate)
    up_value[...] = dot(up_t[...], normed_low[...]) * C**-0.5
    hidden[...] = (up_value[...] * gate_each).astype(BF16)
    result = height[...] + dot(down_t[...], hidden[...]) * FFH**-0.5
    result = result.astype(BF16)
    for col in range(HARM):
        output_ref[:, lanes(col)] = result[:, lanes(col, atoms_n)].T
    grad_hidden = dot(down_w[...], cot_t[...]) * FFH**-0.5
    grad_up[...] = (grad_hidden * gate_each).astype(BF16)
    gate_sum = grad_hidden * up_value[...]
    gate_sum = sum(gate_sum[:, lanes(col, atoms_n)] for col in range(HARM))
    grad_gate = (gate_sum * gate * (1.0 - gate)).astype(BF16)
    along = dot(up_w[...], grad_up[...]) * C**-0.5
    gate_along = dot(gate_w[...], grad_gate) * C**-0.5
    along = jnp.concatenate([along[:, 0:atoms_n] + gate_along, along[:, atoms_n:]], axis=1)
    overlap = atom_sum(along * height[...]) * (inverse * (1.0 / (HARM * C)))
    height_grad[...] = cot_t[...].astype(F32) + each(inverse) * (
        along - height[...] * each(inverse * overlap)
    )

    for k in range(K):
        here = lanes(k, atoms_n)
        gain = jnp.broadcast_to(gains[k : k + 1, :], (SUB, atoms_n))
        turns = turns_of(turn, k, [gain] * HARM)

        def rotate_grads(first, here=here, turns=turns):
            halves = []
            for start in (0, SUB):
                target = pl.ds(pl.multiple_of(first + start, SUB), SUB)
                values = [height_grad[target, lanes(col, atoms_n)] for col in range(HARM)]
                halves.append(
                    [
                        sum(turns[row, col] * values[col] for col in cols_of[row])
                        for row in range(HARM)
                    ]
                )
            for row in range(HARM):
                pair = jnp.concatenate([halves[0][row], halves[1][row]], axis=0)
                grad_mixed[rows_at(row, first, 2 * SUB), here] = pair.astype(BF16)

        over_channels(rotate_grads)
    boost = grad_boost * all_atoms**-0.5

    def pack_piece(piece, rows, width, value):
        for part in range(width):
            packed[pl.ds(piece_start[piece] + part, rows, stride=width), :] = value[:, lanes(part)]

    def weight_grad(left, right, scale):
        return dot(left, right, 1, 1) * (scale * boost)

    zero_grad = weight_grad(rotated[0:ZERO, :], grad_mixed[0:ZERO, :], row_scale[0])
    pack_piece(0, ZERO, 3, zero_grad)
    one_grad = weight_grad(rotated[one_rows, :], grad_mixed[one_rows, :], row_scale[3])
    half = 2 * C
    pack_piece(1, half, 2, one_grad[:half, :half] + one_grad[half:, half:])
    pack_piece(2, half, 2, one_grad[:half, half:] - one_grad[half:, :half])
    two_grad = weight_grad(rotated[two_rows, :], grad_mixed[two_rows, :], row_scale[7])
    pack_piece(3, C, 1, two_grad[:C, :C] + two_grad[C:, C:])
    pack_piece(4, C, 1, two_grad[:C, C:] - two_grad[C:, :C])
    pack_piece(5, C, 2, weight_grad(normed_low[:, 0:atoms_n], grad_gate, C**-0.5))
    pack_piece(6, C, 2, weight_grad(normed_low[...], grad_up[...], C**-0.5))
    pack_piece(7, FFH, 1, weight_grad(hidden[...], cot_t[...], FFH**-0.5))
    shard_rows = PACK_ROWS // node_count
    part_rows = shard_rows // edge_parts
    edge_low = lax.axis_index("edge") & (edge_parts - 1)
    bits = node_count.bit_length() - 1
    blocks = []
    for place in range(node_count):
        distance = int(format(place, "b").zfill(bits)[::-1], 2) if bits else 0
        for part in range(edge_parts):
            blocks.append((node ^ distance) * shard_rows + (edge_low ^ part) * part_rows)
    half = len(blocks) // 2
    for number, first in enumerate(blocks):
        values = packed[pl.ds(pl.multiple_of(first, 8), part_rows), :].astype(BF16)
        target = keep_ref if number < half else send_ref
        target[lanes(number % half, part_rows), :] = values


def slot_kernel(slot_ref, zero_w, one_w, two_w, turn, grad_mixed, height_grad, *refs):
    slot_grad_ref, height_rows_ref, mixed, source = refs
    slots_n = slot_grad_ref.shape[0]
    atoms_n = slot_ref.shape[1]
    one_rows = slice(ZERO, ZERO + ONE)
    two_rows = slice(ZERO + ONE, HARM * C)
    mixed[0:ZERO, :] = dot(zero_w[...], grad_mixed[0:ZERO, :])
    mixed[one_rows, :] = dot(one_w[...], grad_mixed[one_rows, :])
    mixed[two_rows, :] = dot(two_w[...], grad_mixed[two_rows, :])
    for k in range(K):
        here = lanes(k, atoms_n)
        turns = turns_of(turn, k, row_scale)

        def rotate_back(first, here=here, turns=turns):
            for start in (0, SUB):
                values = [mixed[rows_at(row, first + start), here] for row in range(HARM)]
                for col in range(HARM):
                    source[rows_at(col, first + start), here] = sum(
                        turns[row, col] * values[row] for row in rows_of[col]
                    )

        over_channels(rotate_back)
    slot_range = lax.broadcasted_iota(jnp.int32, (slots_n, atoms_n), 0)
    taken = jnp.concatenate(
        [as_low(slot_range == slot_ref[k : k + 1, :]) for k in range(K)], axis=1
    )
    pieces = split_parts(source[...], 3)
    slot_grad_ref[...] = sum(dot(taken, piece, 1, 1) for piece in pieces)
    for col in range(HARM):
        height_rows_ref[:, lanes(col)] = height_grad[:, lanes(col, atoms_n)].T


def finish_kernel(sends_ref, height_rows_ref, back_ref, grad_ref):
    shape = (grad_ref.shape[0], sends_ref.shape[1])
    picks = as_low(lax.broadcasted_iota(jnp.int32, shape, 0) == sends_ref[...])
    pieces = split_parts(back_ref[...], 3)
    total = sum(dot(picks, piece) for piece in pieces)
    grad_ref[...] = (height_rows_ref[...] + total).astype(BF16)


def adam_step(params, moment_one, moment_two, gradient):
    new_one = first_beta * moment_one + (1.0 - first_beta) * gradient
    new_two = second_beta * moment_two + (1.0 - second_beta) * gradient * gradient
    corrected = (
        new_one
        / (1.0 - first_beta**step_count)
        / (jnp.sqrt(new_two / (1.0 - second_beta**step_count)) + adam_epsilon)
    )
    return (params - learn_rate * (corrected + decay_rate * params), new_one, new_two)


def swap(value, axis, bit):
    size = lax.axis_size(axis)
    return lax.ppermute(value, axis, [(i, i ^ (1 << bit)) for i in range(size)])


def shards(
    atoms,
    cotangent,
    params,
    adam_m,
    adam_v,
    sends,
    edge_slot,
    rot_index,
    rot_table,
    edge_gain,
    live_tiles,
):
    node_size = lax.axis_size("node")
    edge_size = lax.axis_size("edge")
    node_bits = node_size.bit_length() - 1
    edge_bits = edge_size.bit_length() - 1
    atoms_n, features = atoms.shape
    slots_n = sends.shape[-1]
    per_peer = slots_n // edge_size
    edges_n = atoms_n * K
    edge_parts = 2 if edge_bits else 1
    vmem = pl.BlockSpec(memory_space=pltpu.VMEM)
    smem = pl.BlockSpec(memory_space=pltpu.SMEM)

    own = params.reshape(-1, C).astype(BF16)
    by_distance = {0: own}
    with jax.named_scope("weights"):
        for bit in reversed(range(node_bits)):
            for distance in list(by_distance):
                with jax.named_scope(f"hop{bit}"):
                    by_distance[distance | (1 << bit)] = swap(by_distance[distance], "node", bit)
    shard_list = [by_distance[distance] for distance in range(node_size)]

    def call(kernel, outs, ins, name, scratch=(), scalars=0):
        return pl.pallas_call(
            kernel,
            out_shape=tuple(jax.ShapeDtypeStruct(*out) for out in outs),
            in_specs=[smem] * scalars + [vmem] * (len(ins) - scalars),
            out_specs=(vmem,) * len(outs),
            scratch_shapes=[pltpu.VMEM(*part) for part in scratch],
            name=name,
        )(*ins)

    def peers_exchange(value):
        value = value.reshape(edge_size, per_peer, features)
        value = lax.all_to_all(value, "edge", split_axis=0, concat_axis=0, tiled=True)
        return value.reshape(slots_n, features)

    send_rows = sends.reshape(1, slots_n)
    slots_t, index_t, gains_t = edge_slot.T, rot_index.T, edge_gain.T
    table_t = jnp.transpose(rot_table, (1, 2, 0)).reshape(HARM * HARM, ROTS)
    wide = HARM * atoms_n
    with jax.named_scope("pick"):
        (outgoing,) = call(pick_kernel, [((slots_n, features), BF16)], (send_rows, atoms), "pick")
    with jax.named_scope("rows"):
        slot_rows = peers_exchange(outgoing)
    with jax.named_scope("prepare"):
        prepared = call(
            functools.partial(prepare_kernel, node_size),
            [
                ((ZERO, ZERO), BF16),
                ((ONE, ONE), BF16),
                ((TWO, TWO), BF16),
                ((ZERO, ZERO), BF16),
                ((ONE, ONE), BF16),
                ((TWO, TWO), BF16),
                ((C, FFH), BF16),
                ((C, FFH), BF16),
                ((FFH, C), BF16),
                ((FFH, C), BF16),
                ((FFH, C), BF16),
                ((C, FFH), BF16),
                ((C, wide), BF16),
                ((C, wide), BF16),
                ((K * TURN_ROWS, atoms_n), F32),
            ],
            (atoms, cotangent, index_t, table_t, *shard_list),
            "prepare",
            [((PACK_ROWS, C), F32)],
        )
    with jax.named_scope("layer"):
        output, height_grad, grad_mixed, keep, send = call(
            functools.partial(main_kernel, edge_parts, node_size, atoms_n * node_size * edge_size),
            [
                ((atoms_n, features), BF16),
                ((C, wide), F32),
                ((features, edges_n), BF16),
                ((PACK_ROWS // 2, C), BF16),
                ((PACK_ROWS // 2, C), BF16),
            ],
            (live_tiles, slot_rows, slots_t, gains_t, *prepared[3:]),
            "layer",
            [
                ((features, edges_n), F32),
                ((features, edges_n), BF16),
                ((features, edges_n), F32),
                ((C, wide), F32),
                ((C, wide), BF16),
                ((FFH, wide), F32),
                ((FFH, wide), BF16),
                ((FFH, wide), BF16),
                ((PACK_ROWS, C), F32),
            ],
            scalars=1,
        )
    with jax.named_scope("slots"):
        slot_grad, height_rows = call(
            slot_kernel,
            [((slots_n, features), F32), ((atoms_n, features), F32)],
            (slots_t, *prepared[:3], prepared[-1], grad_mixed, height_grad),
            "slots",
            [((features, edges_n), F32), ((features, edges_n), F32)],
        )

    def add_low(left, right):
        return (left.astype(F32) + right.astype(F32)).astype(BF16)

    hops = [("node", bit) for bit in range(node_bits)] + [("edge", 0)] * (edge_parts - 1)
    for number, (axis, bit) in enumerate(hops):
        if number:
            half = keep.shape[0] // 2
            keep, send = keep[:half], keep[half:]
        with jax.named_scope(f"grads_{axis}{bit}"):
            keep = add_low(keep, swap(send, axis, bit))
    grads = keep
    for bit in range(1, edge_bits):
        with jax.named_scope(f"grads_edge{bit}"):
            grads = add_low(grads, swap(grads, "edge", bit))
    if edge_bits:
        with jax.named_scope("grads_back"):
            other = swap(grads, "edge", 0)
        is_low = (lax.axis_index("edge") & 1) == 0
        grads = jnp.concatenate(
            [jnp.where(is_low, grads, other), jnp.where(is_low, other, grads)], axis=0
        )

    with jax.named_scope("back"):
        returned = peers_exchange(slot_grad)
    with jax.named_scope("finish"):
        (grad_atoms,) = call(
            finish_kernel,
            [((atoms_n, features), BF16)],
            (send_rows, height_rows, returned),
            "finish",
        )

    def rows_of_lanes(value):
        return value.reshape(-1, C)

    new_params, new_one, new_two = adam_step(
        rows_of_lanes(params), rows_of_lanes(adam_m), rows_of_lanes(adam_v), grads.astype(F32)
    )
    return (
        output,
        grad_atoms,
        new_params.reshape(-1),
        new_one.reshape(-1),
        new_two.reshape(-1),
    )


def solution(mesh):
    return jax.shard_map(
        shards,
        mesh=mesh,
        in_specs=(
            P(("node", "edge"), None),
            P(("node", "edge"), None),
            P("node"),
            P("node"),
            P("node"),
            P("node", "edge", None),
            P(("node", "edge"), None),
            P(("node", "edge"), None),
            P(),
            P(("node", "edge"), None),
            P("node", "edge"),
        ),
        out_specs=(
            P(("node", "edge"), None),
            P(("node", "edge"), None),
            P("node"),
            P("node"),
            P("node"),
        ),
        check_vma=False,
    )
```

```python
import functools

import jax
import jax.numpy as jnp
from jax import lax
from jax.experimental import pallas as pl
from jax.experimental.pallas import tpu as pltpu
from jax.sharding import PartitionSpec as P


C = 128
HARM = 9
FFH = 256
K = 4
TILE_ATOMS = 32
ROTS = 64
SUB = 8
TURN_ROWS = 88

harmonic_order = (0, 2, 6, 3, 7, 1, 5, 8, 4)
norm_epsilon = 1e-06
first_beta = 0.8
second_beta = 0.95
step_count = 100
learn_rate = 0.01
decay_rate = 0.01
adam_epsilon = 1e-08
grad_boost = 4.0

F32 = jnp.float32
BF16 = jnp.bfloat16

degree_block = (0, 1, 1, 1, 2, 2, 2, 2, 2)
entries = [
    (row, col, harmonic_order[row] * HARM + col)
    for row in range(HARM)
    for col in range(HARM)
    if degree_block[harmonic_order[row]] == degree_block[col]
]
cols_of = [[col for r, col, _ in entries if r == row] for row in range(HARM)]
rows_of = [[row for row, c, _ in entries if c == col] for col in range(HARM)]

ZERO, ONE, TWO = 3 * C, 4 * C, 2 * C
row_scale = [ZERO**-0.5] * 3 + [ONE**-0.5] * 4 + [TWO**-0.5] * 2
piece_rows = [9 * C, 4 * C, 4 * C, C, C, 2 * C, 2 * C, 2 * C]
piece_start = [sum(piece_rows[:i]) for i in range(len(piece_rows))]
PACK_ROWS = sum(piece_rows)


def lanes(number, width=C):
    return slice(number * width, (number + 1) * width)


def dot(left, right, left_dim=1, right_dim=0):
    return lax.dot_general(
        left, right, (((left_dim,), (right_dim,)), ((), ())), preferred_element_type=F32
    )


def split_parts(value, count):
    parts = []
    for _ in range(count):
        part = value.astype(BF16)
        parts.append(part)
        value = value - part.astype(F32)
    return parts


def as_low(mask):
    return jnp.where(mask, 1.0, 0.0).astype(BF16)


def pick_kernel(sends_ref, atoms_ref, rows_ref):
    shape = (atoms_ref.shape[0], sends_ref.shape[1])
    picks = as_low(lax.broadcasted_iota(jnp.int32, shape, 0) == sends_ref[...])
    rows_ref[...] = dot(picks, atoms_ref[...], 0, 0).astype(BF16)


def prepare_kernel(node_count, *refs):
    live_ref, atoms_ref, cot_ref, index_ref, slot_ref, gain_ref, table_ref = refs[:7]
    shard_refs = refs[7 : 7 + node_count]
    (
        zero_ref,
        one_ref,
        two_ref,
        zero_t_ref,
        one_t_ref,
        two_t_ref,
        gate_ref,
        up_ref,
        down_ref,
        gate_t_ref,
        up_t_ref,
        down_t_ref,
        atoms_t_ref,
        cot_t_ref,
        turn_ref,
        slot_out_ref,
        gain_out_ref,
        packed,
    ) = refs[7 + node_count :]
    atoms_n = atoms_ref.shape[0]
    slot_out_ref[...] = slot_ref[...]
    is_live = lax.broadcasted_iota(jnp.int32, (K, atoms_n), 1) < live_ref[0, 0] * TILE_ATOMS
    gain_out_ref[...] = jnp.where(is_live, gain_ref[...], 0.0) * K**-0.5
    node = lax.axis_index("node")

    shard_rows = PACK_ROWS // node_count
    for distance in range(node_count):
        first = pl.multiple_of((node ^ distance) * shard_rows, 8)
        packed[pl.ds(first, shard_rows), :] = shard_refs[distance][...].astype(F32)

    def unpack(piece, rows, width, *targets):
        for part in range(width):
            first = piece_start[piece] + part
            block = packed[pl.ds(first, rows, stride=width), :].astype(BF16)
            for target, turned, row, col, sign in targets:
                value = block if sign > 0 else -block
                if turned:
                    target[col + part * C : col + (part + 1) * C, row : row + rows] = value.T
                else:
                    target[row : row + rows, col + part * C : col + (part + 1) * C] = value

    half = 2 * C
    unpack(0, ZERO, 3, (zero_ref, False, 0, 0, 1), (zero_t_ref, True, 0, 0, 1))
    for piece, (matrix, turned, rows) in (
        (1, (one_ref, one_t_ref, half)),
        (3, (two_ref, two_t_ref, C)),
    ):
        width = rows // C
        unpack(
            piece,
            rows,
            width,
            (matrix, False, 0, 0, 1),
            (matrix, False, rows, rows, 1),
            (turned, True, 0, 0, 1),
            (turned, True, rows, rows, 1),
        )
        unpack(
            piece + 1,
            rows,
            width,
            (matrix, False, 0, rows, 1),
            (matrix, False, rows, 0, -1),
            (turned, True, 0, rows, 1),
            (turned, True, rows, 0, -1),
        )
    unpack(5, C, 2, (gate_ref, False, 0, 0, 1), (gate_t_ref, True, 0, 0, 1))
    unpack(6, C, 2, (up_ref, False, 0, 0, 1), (up_t_ref, True, 0, 0, 1))
    unpack(7, FFH, 1, (down_ref, False, 0, 0, 1), (down_t_ref, True, 0, 0, 1))

    for col in range(HARM):
        atoms_t_ref[:, lanes(col, atoms_n)] = atoms_ref[:, lanes(col)].T
        cot_t_ref[:, lanes(col, atoms_n)] = cot_ref[:, lanes(col)].T
    pieces = split_parts(table_ref[...], 3)
    range_of_table = lax.broadcasted_iota(jnp.int32, (ROTS, atoms_n), 0)
    for k in range(K):
        chosen = as_low(range_of_table == index_ref[k : k + 1, :])
        turn_ref[pl.ds(k * TURN_ROWS, HARM * HARM), :] = sum(dot(piece, chosen) for piece in pieces)


def turns_of(turn_ref, k, factors=None):
    values = {}
    for row, col, entry in entries:
        value = turn_ref[pl.ds(k * TURN_ROWS + entry, SUB, stride=0), :]
        values[row, col] = value if factors is None else value * factors[row]
    return values


def over_channels(body):
    def step(number, carry):
        body(pl.multiple_of(number * 2 * SUB, 2 * SUB))
        return carry

    lax.fori_loop(0, C // (2 * SUB), step, 0)


def rows_at(harmonic, first, count=SUB):
    return pl.ds(pl.multiple_of(harmonic * C + first, SUB), count)


def main_kernel(edge_parts, node_count, all_atoms, *refs):
    rows_ref = refs[0]
    sides = refs[1:18]
    output_ref, height_grad, grad_mixed, keep_ref, send_ref, *kept = refs[18:28]
    held = (*refs[28:40], *kept)
    (gain_ref, zero_t, one_t, two_t, gate_w, up_w, down_w, gate_t, up_t, down_t, atoms_t, cot_t) = (
        held[:12]
    )
    slot_ref, turn = kept[:2]
    (
        output_rows,
        arrived,
        source,
        rotated,
        mixed,
        height,
        normed_low,
        up_value,
        hidden,
        grad_up,
        packed,
    ) = refs[40:]
    copies = [
        pltpu.make_async_copy(side, target, arrived.at[number])
        for number, (side, target) in enumerate(zip(sides, held))
    ]
    early, late = [copies[i] for i in (12, 13, 0)], copies[1:12] + copies[14:]
    for copy in early + late:
        copy.start()
    output_copy = pltpu.make_async_copy(output_rows, output_ref, arrived.at[len(copies)])
    atoms_n = output_ref.shape[0]
    slots_n = rows_ref.shape[0]
    node = lax.axis_index("node")

    slot_range = lax.broadcasted_iota(jnp.int32, (slots_n, atoms_n), 0)
    for copy in early:
        copy.wait()
    for k in range(K):
        taken = as_low(slot_range == slot_ref[k : k + 1, :])
        source[:, lanes(k, atoms_n)] = dot(rows_ref[...], taken, 0, 0)
    gains = gain_ref[...]

    for k in range(K):
        here = lanes(k, atoms_n)
        turns = turns_of(turn, k)

        def rotate(first, here=here, turns=turns):
            halves = []
            for start in (0, SUB):
                values = [source[rows_at(col, first + start), here] for col in range(HARM)]
                halves.append(
                    [
                        sum(turns[row, col] * values[col] for col in cols_of[row])
                        for row in range(HARM)
                    ]
                )
            for row in range(HARM):
                pair = jnp.concatenate([halves[0][row], halves[1][row]], axis=0)
                rotated[rows_at(row, first, 2 * SUB), here] = pair.astype(BF16)

        over_channels(rotate)
    for copy in late:
        copy.wait()
    one_rows = slice(ZERO, ZERO + ONE)
    two_rows = slice(ZERO + ONE, HARM * C)
    mixed[0:ZERO, :] = dot(zero_t[...], rotated[0:ZERO, :])
    mixed[one_rows, :] = dot(one_t[...], rotated[one_rows, :])
    mixed[two_rows, :] = dot(two_t[...], rotated[two_rows, :])

    for k in range(K):
        here = lanes(k, atoms_n)
        gain = jnp.broadcast_to(gains[k : k + 1, :], (SUB, atoms_n))
        turns = turns_of(turn, k, [gain * scale for scale in row_scale])

        def gather_messages(first, k=k, here=here, turns=turns):
            if k == 0:
                starts = [
                    atoms_t[pl.ds(first, 2 * SUB), lanes(col, atoms_n)].astype(F32)
                    for col in range(HARM)
                ]
            for start in (0, SUB):
                values = [mixed[rows_at(row, first + start), here] for row in range(HARM)]
                target = pl.ds(pl.multiple_of(first + start, SUB), SUB)
                for col in range(HARM):
                    there = lanes(col, atoms_n)
                    base = starts[col][start : start + SUB] if k == 0 else height[target, there]
                    total = sum(turns[row, col] * values[row] for row in rows_of[col])
                    height[target, there] = base + total

        over_channels(gather_messages)

    def atom_sum(value):
        total = sum(value[:, lanes(col, atoms_n)] for col in range(HARM))
        return jnp.sum(total, axis=0, keepdims=True)

    def each(value):
        return jnp.concatenate([value] * HARM, axis=1)

    mean = atom_sum(height[...] * height[...]) * (1.0 / (HARM * C))
    inverse = lax.rsqrt(mean + norm_epsilon)
    normed_low[...] = (height[...] * each(inverse)).astype(BF16)
    gate = jax.nn.sigmoid(dot(gate_t[...], normed_low[:, 0:atoms_n]) * C**-0.5)
    gate_each = each(gate)
    up_value[...] = dot(up_t[...], normed_low[...]) * C**-0.5
    hidden[...] = (up_value[...] * gate_each).astype(BF16)
    result = height[...] + dot(down_t[...], hidden[...]) * FFH**-0.5
    result = result.astype(BF16)
    for col in range(HARM):
        output_rows[:, lanes(col)] = result[:, lanes(col, atoms_n)].T
    output_copy.start()
    grad_hidden = dot(down_w[...], cot_t[...]) * FFH**-0.5
    grad_up[...] = (grad_hidden * gate_each).astype(BF16)
    gate_sum = grad_hidden * up_value[...]
    gate_sum = sum(gate_sum[:, lanes(col, atoms_n)] for col in range(HARM))
    grad_gate = (gate_sum * gate * (1.0 - gate)).astype(BF16)
    along = dot(up_w[...], grad_up[...]) * C**-0.5
    gate_along = dot(gate_w[...], grad_gate) * C**-0.5
    along = jnp.concatenate([along[:, 0:atoms_n] + gate_along, along[:, atoms_n:]], axis=1)
    overlap = atom_sum(along * height[...]) * (inverse * (1.0 / (HARM * C)))
    height_grad[...] = cot_t[...].astype(F32) + each(inverse) * (
        along - height[...] * each(inverse * overlap)
    )

    for k in range(K):
        here = lanes(k, atoms_n)
        gain = jnp.broadcast_to(gains[k : k + 1, :], (SUB, atoms_n))
        turns = turns_of(turn, k, [gain] * HARM)

        def rotate_grads(first, here=here, turns=turns):
            halves = []
            for start in (0, SUB):
                target = pl.ds(pl.multiple_of(first + start, SUB), SUB)
                values = [height_grad[target, lanes(col, atoms_n)] for col in range(HARM)]
                halves.append(
                    [
                        sum(turns[row, col] * values[col] for col in cols_of[row])
                        for row in range(HARM)
                    ]
                )
            for row in range(HARM):
                pair = jnp.concatenate([halves[0][row], halves[1][row]], axis=0)
                grad_mixed[rows_at(row, first, 2 * SUB), here] = pair.astype(BF16)

        over_channels(rotate_grads)
    boost = grad_boost * all_atoms**-0.5

    def pack_piece(piece, rows, width, value):
        for part in range(width):
            packed[pl.ds(piece_start[piece] + part, rows, stride=width), :] = value[:, lanes(part)]

    def weight_grad(left, right, scale):
        return dot(left, right, 1, 1) * (scale * boost)

    zero_grad = weight_grad(rotated[0:ZERO, :], grad_mixed[0:ZERO, :], row_scale[0])
    pack_piece(0, ZERO, 3, zero_grad)
    one_grad = weight_grad(rotated[one_rows, :], grad_mixed[one_rows, :], row_scale[3])
    half = 2 * C
    pack_piece(1, half, 2, one_grad[:half, :half] + one_grad[half:, half:])
    pack_piece(2, half, 2, one_grad[:half, half:] - one_grad[half:, :half])
    two_grad = weight_grad(rotated[two_rows, :], grad_mixed[two_rows, :], row_scale[7])
    pack_piece(3, C, 1, two_grad[:C, :C] + two_grad[C:, C:])
    pack_piece(4, C, 1, two_grad[:C, C:] - two_grad[C:, :C])
    pack_piece(5, C, 2, weight_grad(normed_low[:, 0:atoms_n], grad_gate, C**-0.5))
    pack_piece(6, C, 2, weight_grad(normed_low[...], grad_up[...], C**-0.5))
    pack_piece(7, FFH, 1, weight_grad(hidden[...], cot_t[...], FFH**-0.5))
    shard_rows = PACK_ROWS // node_count
    part_rows = shard_rows // edge_parts
    edge_low = lax.axis_index("edge") & (edge_parts - 1)
    bits = node_count.bit_length() - 1
    blocks = []
    for place in range(node_count):
        distance = int(format(place, "b").zfill(bits)[::-1], 2) if bits else 0
        for part in range(edge_parts):
            blocks.append((node ^ distance) * shard_rows + (edge_low ^ part) * part_rows)
    half = len(blocks) // 2
    for number, first in enumerate(blocks):
        values = packed[pl.ds(pl.multiple_of(first, 8), part_rows), :].astype(BF16)
        target = keep_ref if number < half else send_ref
        target[lanes(number % half, part_rows), :] = values
    output_copy.wait()


def slot_kernel(slot_ref, turn, zero_w, one_w, two_w, grad_mixed, height_grad, *refs):
    slot_grad_ref, height_rows_ref, mixed, source, slot_rows, arrived = refs
    slots_n = slot_grad_ref.shape[0]
    atoms_n = slot_ref.shape[1]
    one_rows = slice(ZERO, ZERO + ONE)
    two_rows = slice(ZERO + ONE, HARM * C)
    mixed[0:ZERO, :] = dot(zero_w[...], grad_mixed[0:ZERO, :])
    mixed[one_rows, :] = dot(one_w[...], grad_mixed[one_rows, :])
    mixed[two_rows, :] = dot(two_w[...], grad_mixed[two_rows, :])
    for k in range(K):
        here = lanes(k, atoms_n)
        turns = turns_of(turn, k, row_scale)

        def rotate_back(first, here=here, turns=turns):
            for start in (0, SUB):
                values = [mixed[rows_at(row, first + start), here] for row in range(HARM)]
                for col in range(HARM):
                    source[rows_at(col, first + start), here] = sum(
                        turns[row, col] * values[row] for row in rows_of[col]
                    )

        over_channels(rotate_back)
    slot_range = lax.broadcasted_iota(jnp.int32, (slots_n, atoms_n), 0)
    taken = jnp.concatenate(
        [as_low(slot_range == slot_ref[k : k + 1, :]) for k in range(K)], axis=1
    )
    pieces = split_parts(source[...], 3)
    slot_rows[...] = sum(dot(taken, piece, 1, 1) for piece in pieces)
    slot_copy = pltpu.make_async_copy(slot_rows, slot_grad_ref, arrived)
    slot_copy.start()
    for col in range(HARM):
        height_rows_ref[:, lanes(col)] = height_grad[:, lanes(col, atoms_n)].T
    slot_copy.wait()


def finish_kernel(sends_ref, height_rows_ref, back_ref, grad_ref):
    shape = (grad_ref.shape[0], sends_ref.shape[1])
    picks = as_low(lax.broadcasted_iota(jnp.int32, shape, 0) == sends_ref[...])
    pieces = split_parts(back_ref[...], 3)
    total = sum(dot(picks, piece) for piece in pieces)
    grad_ref[...] = (height_rows_ref[...] + total).astype(BF16)


def adam_step(params, moment_one, moment_two, gradient):
    new_one = first_beta * moment_one + (1.0 - first_beta) * gradient
    new_two = second_beta * moment_two + (1.0 - second_beta) * gradient * gradient
    corrected = (
        new_one
        / (1.0 - first_beta**step_count)
        / (jnp.sqrt(new_two / (1.0 - second_beta**step_count)) + adam_epsilon)
    )
    return (params - learn_rate * (corrected + decay_rate * params), new_one, new_two)


def swap(value, axis, bit):
    size = lax.axis_size(axis)
    return lax.ppermute(value, axis, [(i, i ^ (1 << bit)) for i in range(size)])


def shards(
    atoms,
    cotangent,
    params,
    adam_m,
    adam_v,
    sends,
    edge_slot,
    rot_index,
    rot_table,
    edge_gain,
    live_tiles,
):
    node_size = lax.axis_size("node")
    edge_size = lax.axis_size("edge")
    node_bits = node_size.bit_length() - 1
    edge_bits = edge_size.bit_length() - 1
    atoms_n, features = atoms.shape
    slots_n = sends.shape[-1]
    per_peer = slots_n // edge_size
    edges_n = atoms_n * K
    edge_parts = 2 if edge_bits else 1

    own = params.reshape(-1, C).astype(BF16)
    by_distance = {0: own}
    for bit in reversed(range(node_bits)):
        for distance in list(by_distance):
            by_distance[distance | (1 << bit)] = swap(by_distance[distance], "node", bit)
    shard_list = [by_distance[distance] for distance in range(node_size)]

    spaces = {"vmem": pltpu.VMEM, "smem": pltpu.SMEM, "hbm": pltpu.HBM, "auto": pltpu.VMEM}

    def call(kernel, outs, ins, scratch=(), megabytes=None):
        def typed_out(place, shape, dtype):
            if place in ("vmem", "hbm"):
                return spaces[place](shape, dtype)
            return jax.ShapeDtypeStruct(shape, dtype)

        def typed_in(place, value):
            if place in ("vmem", "hbm"):
                return pltpu.with_memory_space_constraint(value, spaces[place])
            return value

        limit = None if megabytes is None else megabytes << 20
        return pl.pallas_call(
            kernel,
            out_shape=tuple(typed_out(*out) for out in outs),
            in_specs=[pl.BlockSpec(memory_space=spaces[place]) for place, _ in ins],
            out_specs=tuple(pl.BlockSpec(memory_space=spaces[out[0]]) for out in outs),
            scratch_shapes=list(scratch),
            compiler_params=pltpu.CompilerParams(vmem_limit_bytes=limit),
        )(*(typed_in(*each_in) for each_in in ins))

    def peers_exchange(value):
        value = value.reshape(edge_size, per_peer, features)
        value = lax.all_to_all(value, "edge", split_axis=0, concat_axis=0, tiled=True)
        return value.reshape(slots_n, features)

    send_rows = sends.reshape(1, slots_n)
    slots_t, index_t, gains_t = edge_slot.T, rot_index.T, edge_gain.T
    table_t = jnp.transpose(rot_table, (1, 2, 0)).reshape(HARM * HARM, ROTS)
    wide = HARM * atoms_n
    (outgoing,) = call(
        pick_kernel, [("auto", (slots_n, features), BF16)], [("auto", send_rows), ("auto", atoms)]
    )
    slot_rows = peers_exchange(outgoing)
    matrix_shapes = [(ZERO, ZERO), (ONE, ONE), (TWO, TWO)]
    side_shapes = matrix_shapes + [(C, FFH)] * 2 + [(FFH, C)] * 3 + [(C, FFH)] + [(C, wide)] * 2
    prepared = call(
        functools.partial(prepare_kernel, node_size),
        [("auto", shape, BF16) for shape in matrix_shapes + side_shapes]
        + [
            ("auto", (K * TURN_ROWS, atoms_n), F32),
            ("auto", (K, atoms_n), jnp.int32),
            ("auto", (K, atoms_n), F32),
        ],
        [("smem", live_tiles)]
        + [("auto", value) for value in (atoms, cotangent, index_t, slots_t, gains_t, table_t)]
        + [("auto", value) for value in shard_list],
        [pltpu.VMEM((PACK_ROWS, C), F32)],
    )
    matrices, sides, (turn, slots_kept, gains_kept) = prepared[:3], prepared[3:-3], prepared[-3:]
    forwarded = (slots_kept, turn, *matrices)
    output, height_grad, grad_mixed, keep, send, *kept = call(
        functools.partial(main_kernel, edge_parts, node_size, atoms_n * node_size * edge_size),
        [
            ("hbm", (atoms_n, features), BF16),
            ("vmem", (C, wide), F32),
            ("vmem", (features, edges_n), BF16),
            ("vmem", (PACK_ROWS // 2, C), BF16),
            ("vmem", (PACK_ROWS // 2, C), BF16),
        ]
        + [("vmem", value.shape, value.dtype) for value in forwarded],
        [("vmem", slot_rows)]
        + [("hbm", value) for value in (gains_kept, *sides, *forwarded)],
        [
            pltpu.VMEM((K, atoms_n), F32),
            *(pltpu.VMEM(shape, BF16) for shape in side_shapes),
            pltpu.VMEM((atoms_n, features), BF16),
            pltpu.SemaphoreType.DMA((len(side_shapes) + len(forwarded) + 2,)),
            pltpu.VMEM((features, edges_n), F32),
            pltpu.VMEM((features, edges_n), BF16),
            pltpu.VMEM((features, edges_n), F32),
            pltpu.VMEM((C, wide), F32),
            pltpu.VMEM((C, wide), BF16),
            pltpu.VMEM((FFH, wide), F32),
            pltpu.VMEM((FFH, wide), BF16),
            pltpu.VMEM((FFH, wide), BF16),
            pltpu.VMEM((PACK_ROWS, C), F32),
        ],
        megabytes=28,
    )
    slot_grad, height_rows = call(
        slot_kernel,
        [("hbm", (slots_n, features), F32), ("vmem", (atoms_n, features), F32)],
        [
            ("vmem", value)
            for value in (*kept, grad_mixed, height_grad)
        ],
        [
            pltpu.VMEM((features, edges_n), F32),
            pltpu.VMEM((features, edges_n), F32),
            pltpu.VMEM((slots_n, features), F32),
            pltpu.SemaphoreType.DMA,
        ],
        megabytes=20,
    )

    def add_low(left, right):
        return (left.astype(F32) + right.astype(F32)).astype(BF16)

    hops = [("node", bit) for bit in range(node_bits)] + [("edge", 0)] * (edge_parts - 1)
    for number, (axis, bit) in enumerate(hops):
        if number:
            half = keep.shape[0] // 2
            keep, send = keep[:half], keep[half:]
        keep = add_low(keep, swap(send, axis, bit))
    grads = keep
    for bit in range(1, edge_bits):
        grads = add_low(grads, swap(grads, "edge", bit))
    if edge_bits:
        other = swap(grads, "edge", 0)
        is_low = (lax.axis_index("edge") & 1) == 0
        grads = jnp.concatenate(
            [jnp.where(is_low, grads, other), jnp.where(is_low, other, grads)], axis=0
        )

    returned = peers_exchange(slot_grad)
    (grad_atoms,) = call(
        finish_kernel,
        [("auto", (atoms_n, features), BF16)],
        [("auto", send_rows), ("vmem", height_rows), ("vmem", returned)],
        megabytes=8,
    )

    def rows_of_lanes(value):
        return value.reshape(-1, C)

    new_params, new_one, new_two = adam_step(
        rows_of_lanes(params), rows_of_lanes(adam_m), rows_of_lanes(adam_v), grads.astype(F32)
    )
    return (
        output,
        grad_atoms,
        new_params.reshape(-1),
        new_one.reshape(-1),
        new_two.reshape(-1),
    )


def solution(mesh):
    return jax.shard_map(
        shards,
        mesh=mesh,
        in_specs=(
            P(("node", "edge"), None),
            P(("node", "edge"), None),
            P("node"),
            P("node"),
            P("node"),
            P("node", "edge", None),
            P(("node", "edge"), None),
            P(("node", "edge"), None),
            P(),
            P(("node", "edge"), None),
            P("node", "edge"),
        ),
        out_specs=(
            P(("node", "edge"), None),
            P(("node", "edge"), None),
            P("node"),
            P("node"),
            P("node"),
        ),
        check_vma=False,
    )
```

```python
import functools

import jax
import jax.numpy as jnp
from jax import lax
from jax.experimental import pallas as pl
from jax.experimental.pallas import tpu as pltpu
from jax.sharding import PartitionSpec as P


C = 128
HARM = 9
FFH = 256
K = 4
TILE_ATOMS = 32
ROTS = 64
SUB = 8
TURN_ROWS = 88
GROUPS = 2

harmonic_order = (0, 2, 6, 3, 7, 1, 5, 8, 4)
norm_epsilon = 1e-06
first_beta = 0.8
second_beta = 0.95
step_count = 100
learn_rate = 0.01
decay_rate = 0.01
adam_epsilon = 1e-08
grad_boost = 4.0

F32 = jnp.float32
BF16 = jnp.bfloat16

degree_block = (0, 1, 1, 1, 2, 2, 2, 2, 2)
entries = [
    (row, col, harmonic_order[row] * HARM + col)
    for row in range(HARM)
    for col in range(HARM)
    if degree_block[harmonic_order[row]] == degree_block[col]
]
cols_of = [[col for r, col, _ in entries if r == row] for row in range(HARM)]
rows_of = [[row for row, c, _ in entries if c == col] for col in range(HARM)]

ZERO, ONE, TWO = 3 * C, 4 * C, 2 * C
row_scale = [ZERO**-0.5] * 3 + [ONE**-0.5] * 4 + [TWO**-0.5] * 2
piece_rows = [9 * C, 4 * C, 4 * C, C, C, 2 * C, 2 * C, 2 * C]
piece_start = [sum(piece_rows[:i]) for i in range(len(piece_rows))]
PACK_ROWS = sum(piece_rows)


def lanes(number, width=C):
    return slice(number * width, (number + 1) * width)


def dot(left, right, left_dim=1, right_dim=0):
    return lax.dot_general(
        left, right, (((left_dim,), (right_dim,)), ((), ())), preferred_element_type=F32
    )


def split_parts(value, count):
    parts = []
    for _ in range(count):
        part = value.astype(BF16)
        parts.append(part)
        value = value - part.astype(F32)
    return parts


def as_low(mask):
    return jnp.where(mask, 1.0, 0.0).astype(BF16)


def pick_kernel(sends_ref, atoms_ref, params_ref, rows_ref, own_ref):
    shape = (atoms_ref.shape[0], sends_ref.shape[1])
    picks = as_low(lax.broadcasted_iota(jnp.int32, shape, 0) == sends_ref[...])
    rows_ref[...] = dot(picks, atoms_ref[...], 0, 0).astype(BF16)
    own_ref[...] = params_ref[...].astype(BF16)


def arrange_kernel(live_ref, atoms_ref, cot_ref, index_ref, gain_ref, table_ref, *outs):
    atoms_t_ref, cot_t_ref, turn_ref, gain_out_ref = outs
    atoms_n = atoms_ref.shape[0]
    is_live = lax.broadcasted_iota(jnp.int32, (K, atoms_n), 1) < live_ref[0, 0] * TILE_ATOMS
    gain_out_ref[...] = jnp.where(is_live, gain_ref[...], 0.0) * K**-0.5
    for col in range(HARM):
        atoms_t_ref[:, lanes(col, atoms_n)] = atoms_ref[:, lanes(col)].T
        cot_t_ref[:, lanes(col, atoms_n)] = cot_ref[:, lanes(col)].T
    pieces = split_parts(table_ref[...], 3)
    range_of_table = lax.broadcasted_iota(jnp.int32, (ROTS, atoms_n), 0)
    for k in range(K):
        chosen = as_low(range_of_table == index_ref[k : k + 1, :])
        turn_ref[pl.ds(k * TURN_ROWS, HARM * HARM), :] = sum(dot(piece, chosen) for piece in pieces)


def unpack_kernel(node_count, *refs):
    shard_refs = refs[:node_count]
    out_refs = refs[node_count : node_count + 12]
    built = refs[node_count + 12 : node_count + 24]
    packed, arrived = refs[node_count + 24 :]
    (
        zero_ref,
        one_ref,
        two_ref,
        zero_t_ref,
        one_t_ref,
        two_t_ref,
        gate_ref,
        up_ref,
        down_ref,
        gate_t_ref,
        up_t_ref,
        down_t_ref,
    ) = built
    copies = [
        pltpu.make_async_copy(source, target, arrived.at[number])
        for number, (source, target) in enumerate(zip(built, out_refs))
    ]
    node = lax.axis_index("node")

    shard_rows = PACK_ROWS // node_count
    for distance in range(node_count):
        first = pl.multiple_of((node ^ distance) * shard_rows, 8)
        packed[pl.ds(first, shard_rows), :] = shard_refs[distance][...].astype(F32)

    def unpack(piece, rows, width, *targets):
        for part in range(width):
            first = piece_start[piece] + part
            block = packed[pl.ds(first, rows, stride=width), :].astype(BF16)
            turned_block = block.T
            for target, turned, row, col, sign in targets:
                value = turned_block if turned else block
                value = value if sign > 0 else -value
                if turned:
                    target[col + part * C : col + (part + 1) * C, row : row + rows] = value
                else:
                    target[row : row + rows, col + part * C : col + (part + 1) * C] = value

    half = 2 * C
    unpack(0, ZERO, 3, (zero_t_ref, True, 0, 0, 1), (zero_ref, False, 0, 0, 1))
    copies[3].start()
    copies[0].start()
    for piece, matrix, turned, rows, places in (
        (1, one_ref, one_t_ref, half, (1, 4)),
        (3, two_ref, two_t_ref, C, (2, 5)),
    ):
        width = rows // C
        unpack(
            piece,
            rows,
            width,
            (turned, True, 0, 0, 1),
            (turned, True, rows, rows, 1),
            (matrix, False, 0, 0, 1),
            (matrix, False, rows, rows, 1),
        )
        unpack(
            piece + 1,
            rows,
            width,
            (turned, True, 0, rows, 1),
            (turned, True, rows, 0, -1),
            (matrix, False, 0, rows, 1),
            (matrix, False, rows, 0, -1),
        )
        for place in places:
            copies[place].start()
    unpack(5, C, 2, (gate_ref, False, 0, 0, 1), (gate_t_ref, True, 0, 0, 1))
    unpack(6, C, 2, (up_ref, False, 0, 0, 1), (up_t_ref, True, 0, 0, 1))
    unpack(7, FFH, 1, (down_ref, False, 0, 0, 1), (down_t_ref, True, 0, 0, 1))
    for copy in copies[6:]:
        copy.start()
    for copy in copies:
        copy.wait()


def turns_of(turn_ref, k, factors=None):
    values = {}
    for row, col, entry in entries:
        value = turn_ref[pl.ds(k * TURN_ROWS + entry, SUB, stride=0), :]
        values[row, col] = value if factors is None else value * factors[row]
    return values


def over_channels(body):
    def step(number, carry):
        for part in range(GROUPS):
            body(pl.multiple_of((number * GROUPS + part) * 2 * SUB, 2 * SUB))
        return carry

    lax.fori_loop(0, C // (2 * SUB * GROUPS), step, 0)


def flat(value):
    return value.reshape(value.shape[0] * value.shape[1], value.shape[2])


ZERO_PART, ONE_PART, TWO_PART = slice(0, 3), slice(3, 7), slice(7, 9)


def main_kernel(edge_parts, node_count, all_atoms, *refs):
    rows_ref = refs[0]
    sides = refs[1:15]
    output_ref, height_grad, grad_mixed, keep_ref, send_ref = refs[15:20]
    held = refs[20:34]
    slot_ref, turn, gain_ref = held[:3]
    (zero_t, one_t, two_t, gate_w, up_w, down_w, gate_t, up_t, down_t, atoms_t, cot_t) = held[3:]
    (
        output_rows,
        arrived,
        source,
        rotated,
        mixed,
        height,
        normed_low,
        up_value,
        hidden,
        grad_up,
        packed,
    ) = refs[34:]
    copies = [
        pltpu.make_async_copy(side, target, arrived.at[number])
        for number, (side, target) in enumerate(zip(sides, held))
    ]
    early, late = copies[:3], copies[3:]
    for copy in early + late:
        copy.start()
    output_copy = pltpu.make_async_copy(output_rows, output_ref, arrived.at[len(copies)])
    atoms_n = output_ref.shape[0]
    slots_n = rows_ref.shape[0]
    node = lax.axis_index("node")

    slot_range = lax.broadcasted_iota(jnp.int32, (slots_n, atoms_n), 0)
    for copy in early:
        copy.wait()
    taken = jnp.concatenate(
        [as_low(slot_range == slot_ref[k : k + 1, :]) for k in range(K)], axis=1
    )
    source[...] = dot(rows_ref[...], taken, 0, 0).reshape(source.shape)
    gains = gain_ref[...]

    for k in range(K):
        here = lanes(k, atoms_n)
        turns = turns_of(turn, k)

        def rotate(first, here=here, turns=turns):
            halves = []
            for start in (0, SUB):
                values = [source[col, pl.ds(first + start, SUB), here] for col in range(HARM)]
                halves.append(
                    [
                        sum(turns[row, col] * values[col] for col in cols_of[row])
                        for row in range(HARM)
                    ]
                )
            for row in range(HARM):
                pair = jnp.concatenate([halves[0][row], halves[1][row]], axis=0)
                rotated[row, pl.ds(first, 2 * SUB), here] = pair.astype(BF16)

        over_channels(rotate)
    for copy in late:
        copy.wait()
    for part, matrix in ((ZERO_PART, zero_t), (ONE_PART, one_t), (TWO_PART, two_t)):
        mixed[part] = dot(matrix[...], flat(rotated[part])).reshape(mixed[part].shape)

    for k in range(K):
        here = lanes(k, atoms_n)
        gain = jnp.broadcast_to(gains[k : k + 1, :], (SUB, atoms_n))
        turns = turns_of(turn, k, [gain * scale for scale in row_scale])

        def gather_messages(first, k=k, here=here, turns=turns):
            if k == 0:
                starts = [
                    atoms_t[pl.ds(first, 2 * SUB), lanes(col, atoms_n)].astype(F32)
                    for col in range(HARM)
                ]
            for start in (0, SUB):
                values = [mixed[row, pl.ds(first + start, SUB), here] for row in range(HARM)]
                target = pl.ds(first + start, SUB)
                for col in range(HARM):
                    there = lanes(col, atoms_n)
                    base = starts[col][start : start + SUB] if k == 0 else height[target, there]
                    total = sum(turns[row, col] * values[row] for row in rows_of[col])
                    height[target, there] = base + total

        over_channels(gather_messages)

    def atom_sum(value):
        total = sum(value[:, lanes(col, atoms_n)] for col in range(HARM))
        return jnp.sum(total, axis=0, keepdims=True)

    def each(value):
        return jnp.concatenate([value] * HARM, axis=1)

    mean = atom_sum(height[...] * height[...]) * (1.0 / (HARM * C))
    inverse = lax.rsqrt(mean + norm_epsilon)
    normed_low[...] = (height[...] * each(inverse)).astype(BF16)
    gate = jax.nn.sigmoid(dot(gate_t[...], normed_low[:, 0:atoms_n]) * C**-0.5)
    up_gate, down_gate = gate * C**-0.5, gate * FFH**-0.5
    up_value[...] = dot(up_t[...], normed_low[...])
    for col in range(HARM):
        here = lanes(col, atoms_n)
        hidden[:, here] = (up_value[:, here] * up_gate).astype(BF16)
    projected = dot(down_t[...], hidden[...])
    for col in range(HARM):
        here = lanes(col, atoms_n)
        result = (height[:, here] + projected[:, here] * FFH**-0.5).astype(BF16)
        output_rows[:, lanes(col)] = result.T
    output_copy.start()
    gate_sum = jnp.zeros_like(gate)
    for col in range(HARM):
        here = lanes(col, atoms_n)
        grad_hidden = dot(down_w[...], cot_t[:, here])
        grad_up[:, here] = (grad_hidden * down_gate).astype(BF16)
        gate_sum = gate_sum + grad_hidden * up_value[:, here]
    gate_sum = gate_sum * (C**-0.5 * FFH**-0.5)
    grad_gate = (gate_sum * gate * (1.0 - gate)).astype(BF16)
    along = dot(up_w[...], grad_up[...]) * C**-0.5
    gate_along = dot(gate_w[...], grad_gate) * C**-0.5
    along = jnp.concatenate([along[:, 0:atoms_n] + gate_along, along[:, atoms_n:]], axis=1)
    overlap = atom_sum(along * height[...]) * (inverse * (1.0 / (HARM * C)))
    height_grad[...] = cot_t[...].astype(F32) + each(inverse) * (
        along - height[...] * each(inverse * overlap)
    )

    for k in range(K):
        here = lanes(k, atoms_n)
        gain = jnp.broadcast_to(gains[k : k + 1, :], (SUB, atoms_n))
        turns = turns_of(turn, k, [gain] * HARM)

        def rotate_grads(first, here=here, turns=turns):
            halves = []
            for start in (0, SUB):
                target = pl.ds(first + start, SUB)
                values = [height_grad[target, lanes(col, atoms_n)] for col in range(HARM)]
                halves.append(
                    [
                        sum(turns[row, col] * values[col] for col in cols_of[row])
                        for row in range(HARM)
                    ]
                )
            for row in range(HARM):
                pair = jnp.concatenate([halves[0][row], halves[1][row]], axis=0)
                grad_mixed[row, pl.ds(first, 2 * SUB), here] = pair.astype(BF16)

        over_channels(rotate_grads)
    boost = grad_boost * all_atoms**-0.5

    def pack_piece(piece, rows, width, value):
        for part in range(width):
            packed[pl.ds(piece_start[piece] + part, rows, stride=width), :] = value[:, lanes(part)]

    def weight_grad(left, right, scale):
        return dot(left, right, 1, 1) * (scale * boost)

    zero_grad = weight_grad(flat(rotated[ZERO_PART]), flat(grad_mixed[ZERO_PART]), row_scale[0])
    pack_piece(0, ZERO, 3, zero_grad)
    one_grad = weight_grad(flat(rotated[ONE_PART]), flat(grad_mixed[ONE_PART]), row_scale[3])
    half = 2 * C
    pack_piece(1, half, 2, one_grad[:half, :half] + one_grad[half:, half:])
    pack_piece(2, half, 2, one_grad[:half, half:] - one_grad[half:, :half])
    two_grad = weight_grad(flat(rotated[TWO_PART]), flat(grad_mixed[TWO_PART]), row_scale[7])
    pack_piece(3, C, 1, two_grad[:C, :C] + two_grad[C:, C:])
    pack_piece(4, C, 1, two_grad[:C, C:] - two_grad[C:, :C])
    pack_piece(5, C, 2, weight_grad(normed_low[:, 0:atoms_n], grad_gate, C**-0.5))
    pack_piece(6, C, 2, weight_grad(normed_low[...], grad_up[...], C**-0.5))
    pack_piece(7, FFH, 1, weight_grad(hidden[...], cot_t[...], FFH**-0.5))
    shard_rows = PACK_ROWS // node_count
    part_rows = shard_rows // edge_parts
    edge_low = lax.axis_index("edge") & (edge_parts - 1)
    bits = node_count.bit_length() - 1
    blocks = []
    for place in range(node_count):
        distance = int(format(place, "b").zfill(bits)[::-1], 2) if bits else 0
        for part in range(edge_parts):
            blocks.append((node ^ distance) * shard_rows + (edge_low ^ part) * part_rows)
    half = len(blocks) // 2
    for number, first in enumerate(blocks):
        values = packed[pl.ds(pl.multiple_of(first, 8), part_rows), :].astype(BF16)
        target = keep_ref if number < half else send_ref
        target[lanes(number % half, part_rows), :] = values
    output_copy.wait()


def slot_kernel(grad_mixed, height_grad, *refs):
    sides, held = refs[:5], refs[7:12]
    slot_grad_ref, height_rows_ref = refs[5:7]
    zero_w, one_w, two_w, turn, slot_ref = held
    mixed, source_high, source_low, slot_rows, arrived = refs[12:]
    copies = [
        pltpu.make_async_copy(side, target, arrived.at[number])
        for number, (side, target) in enumerate(zip(sides, held))
    ]
    for copy in copies:
        copy.start()
    slots_n = slot_grad_ref.shape[0]
    atoms_n = slot_ref.shape[1]
    for col in range(HARM):
        height_rows_ref[:, lanes(col)] = height_grad[:, lanes(col, atoms_n)].T
    parts = ((ZERO_PART, zero_w), (ONE_PART, one_w), (TWO_PART, two_w))
    for (part, matrix), copy in zip(parts, copies):
        copy.wait()
        mixed[part] = dot(matrix[...], flat(grad_mixed[part])).reshape(mixed[part].shape)
    for copy in copies[3:]:
        copy.wait()
    for k in range(K):
        here = lanes(k, atoms_n)
        turns = turns_of(turn, k, row_scale)

        def rotate_back(first, here=here, turns=turns):
            halves = []
            for start in (0, SUB):
                values = [mixed[row, pl.ds(first + start, SUB), here] for row in range(HARM)]
                halves.append(
                    [
                        sum(turns[row, col] * values[row] for row in rows_of[col])
                        for col in range(HARM)
                    ]
                )
            for col in range(HARM):
                pair = jnp.concatenate([halves[0][col], halves[1][col]], axis=0)
                for target, part in zip((source_high, source_low), split_parts(pair, 2)):
                    target[col, pl.ds(first, 2 * SUB), here] = part

        over_channels(rotate_back)
    slot_range = lax.broadcasted_iota(jnp.int32, (slots_n, atoms_n), 0)
    taken = jnp.concatenate(
        [as_low(slot_range == slot_ref[k : k + 1, :]) for k in range(K)], axis=1
    )
    slot_rows[...] = dot(taken, flat(source_high[...]), 1, 1) + dot(
        taken, flat(source_low[...]), 1, 1
    )
    slot_copy = pltpu.make_async_copy(slot_rows, slot_grad_ref, arrived.at[len(copies)])
    slot_copy.start()
    slot_copy.wait()


def finish_kernel(sends_ref, height_rows_ref, back_ref, grad_ref):
    shape = (grad_ref.shape[0], sends_ref.shape[1])
    picks = as_low(lax.broadcasted_iota(jnp.int32, shape, 0) == sends_ref[...])
    pieces = split_parts(back_ref[...], 3)
    total = sum(dot(picks, piece) for piece in pieces)
    grad_ref[...] = (height_rows_ref[...] + total).astype(BF16)


def adam_step(params, moment_one, moment_two, gradient):
    new_one = first_beta * moment_one + (1.0 - first_beta) * gradient
    new_two = second_beta * moment_two + (1.0 - second_beta) * gradient * gradient
    corrected = (
        new_one
        / (1.0 - first_beta**step_count)
        / (jnp.sqrt(new_two / (1.0 - second_beta**step_count)) + adam_epsilon)
    )
    return (params - learn_rate * (corrected + decay_rate * params), new_one, new_two)


def swap(value, axis, bit):
    size = lax.axis_size(axis)
    return lax.ppermute(value, axis, [(i, i ^ (1 << bit)) for i in range(size)])


def swap_both(value, node_step, edge_step):
    nodes, edges = lax.axis_size("node"), lax.axis_size("edge")
    pairs = [
        (n * edges + e, (n ^ node_step) * edges + (e ^ edge_step))
        for n in range(nodes)
        for e in range(edges)
    ]
    return lax.ppermute(value, ("node", "edge"), pairs)


def shards(
    atoms,
    cotangent,
    params,
    adam_m,
    adam_v,
    sends,
    edge_slot,
    rot_index,
    rot_table,
    edge_gain,
    live_tiles,
):
    node_size = lax.axis_size("node")
    edge_size = lax.axis_size("edge")
    node_bits = node_size.bit_length() - 1
    edge_bits = edge_size.bit_length() - 1
    atoms_n, features = atoms.shape
    slots_n = sends.shape[-1]
    per_peer = slots_n // edge_size
    edges_n = atoms_n * K
    edge_parts = 2

    spaces = {"vmem": pltpu.VMEM, "smem": pltpu.SMEM, "hbm": pltpu.HBM, "auto": pltpu.VMEM}

    def call(kernel, outs, ins, scratch=(), megabytes=None):
        def typed_out(place, shape, dtype):
            if place in ("vmem", "hbm"):
                return spaces[place](shape, dtype)
            return jax.ShapeDtypeStruct(shape, dtype)

        def typed_in(place, value):
            if place in ("vmem", "hbm"):
                return pltpu.with_memory_space_constraint(value, spaces[place])
            return value

        limit = None if megabytes is None else megabytes << 20
        return pl.pallas_call(
            kernel,
            out_shape=tuple(typed_out(*out) for out in outs),
            in_specs=[pl.BlockSpec(memory_space=spaces[place]) for place, _ in ins],
            out_specs=tuple(pl.BlockSpec(memory_space=spaces[out[0]]) for out in outs),
            scratch_shapes=list(scratch),
            compiler_params=pltpu.CompilerParams(vmem_limit_bytes=limit),
        )(*(typed_in(*each_in) for each_in in ins))

    def peers_exchange(value):
        value = value.reshape(edge_size, per_peer, features)
        value = lax.all_to_all(value, "edge", split_axis=0, concat_axis=0, tiled=True)
        return value.reshape(slots_n, features)

    send_rows = sends.reshape(1, slots_n)
    slots_t, index_t, gains_t = edge_slot.T, rot_index.T, edge_gain.T
    table_t = jnp.transpose(rot_table, (1, 2, 0)).reshape(HARM * HARM, ROTS)
    wide = HARM * atoms_n
    outgoing, own = call(
        pick_kernel,
        [("auto", (slots_n, features), BF16), ("auto", (PACK_ROWS // node_size, C), BF16)],
        [("auto", value) for value in (send_rows, atoms, params.reshape(-1, C))],
    )
    slot_rows = peers_exchange(outgoing)
    by_distance = {0: own}
    for bit in reversed(range(node_bits)):
        for distance in list(by_distance):
            by_distance[distance | (1 << bit)] = swap(by_distance[distance], "node", bit)
    matrix_shapes = [(ZERO, ZERO), (ONE, ONE), (TWO, TWO)]
    unpacked_shapes = matrix_shapes * 2 + [(C, FFH)] * 2 + [(FFH, C)] * 3 + [(C, FFH)]
    atoms_t, cot_t, turn, gains_kept = call(
        arrange_kernel,
        [
            ("auto", (C, wide), BF16),
            ("auto", (C, wide), BF16),
            ("auto", (K * TURN_ROWS, atoms_n), F32),
            ("auto", (K, atoms_n), F32),
        ],
        [("smem", live_tiles)]
        + [("auto", value) for value in (atoms, cotangent, index_t, gains_t, table_t)],
    )
    unpacked = call(
        functools.partial(unpack_kernel, node_size),
        [("hbm", shape, BF16) for shape in unpacked_shapes],
        [("vmem", by_distance[distance]) for distance in range(node_size)],
        [
            *(pltpu.VMEM(shape, BF16) for shape in unpacked_shapes),
            pltpu.VMEM((PACK_ROWS, C), F32),
            pltpu.SemaphoreType.DMA((len(unpacked_shapes),)),
        ],
        megabytes=16,
    )
    sides = (slots_t, turn, gains_kept, *unpacked[3:], atoms_t, cot_t)
    read_again = (*unpacked[:3], turn, slots_t)
    output, height_grad, grad_mixed, keep, send = call(
        functools.partial(main_kernel, edge_parts, node_size, atoms_n * node_size * edge_size),
        [
            ("hbm", (atoms_n, features), BF16),
            ("vmem", (C, wide), F32),
            ("vmem", (HARM, C, edges_n), BF16),
            ("vmem", (PACK_ROWS // 2, C), BF16),
            ("vmem", (PACK_ROWS // 2, C), BF16),
        ],
        [("vmem", slot_rows)]
        + [("hbm", value) for value in sides],
        [
            *(pltpu.VMEM(value.shape, value.dtype) for value in sides),
            pltpu.VMEM((atoms_n, features), BF16),
            pltpu.SemaphoreType.DMA((len(sides) + 1,)),
            pltpu.VMEM((HARM, C, edges_n), F32),
            pltpu.VMEM((HARM, C, edges_n), BF16),
            pltpu.VMEM((HARM, C, edges_n), F32),
            pltpu.VMEM((C, wide), F32),
            pltpu.VMEM((C, wide), BF16),
            pltpu.VMEM((FFH, wide), F32),
            pltpu.VMEM((FFH, wide), BF16),
            pltpu.VMEM((FFH, wide), BF16),
            pltpu.VMEM((PACK_ROWS, C), F32),
        ],
        megabytes=28,
    )
    slot_grad, height_rows = call(
        slot_kernel,
        [("hbm", (slots_n, features), F32), ("vmem", (atoms_n, features), F32)],
        [("vmem", grad_mixed), ("vmem", height_grad)]
        + [("hbm", value) for value in read_again],
        [
            *(pltpu.VMEM(value.shape, value.dtype) for value in read_again),
            pltpu.VMEM((HARM, C, edges_n), F32),
            pltpu.VMEM((HARM, C, edges_n), BF16),
            pltpu.VMEM((HARM, C, edges_n), BF16),
            pltpu.VMEM((slots_n, features), F32),
            pltpu.SemaphoreType.DMA((len(read_again) + 1,)),
        ],
        megabytes=20,
    )

    def add_low(left, right):
        return (left.astype(F32) + right.astype(F32)).astype(BF16)

    for bit in range(node_bits - 1):
        if bit:
            half = keep.shape[0] // 2
            keep, send = keep[:half], keep[half:]
        keep = add_low(keep, swap(send, "node", bit))
    quarter = keep.shape[0] // 4
    total = keep[:quarter].astype(F32)
    for number in (2, 3, 1):
        came = swap_both(
            keep[number * quarter : (number + 1) * quarter],
            (number >> 1) << (node_bits - 1),
            number & 1,
        )
        total = total + came.astype(F32)
    grads = total.astype(BF16)
    for bit in range(1, edge_bits):
        grads = add_low(grads, swap(grads, "edge", bit))
    other = swap(grads, "edge", 0)
    is_low = (lax.axis_index("edge") & 1) == 0
    grads = jnp.concatenate(
        [jnp.where(is_low, grads, other), jnp.where(is_low, other, grads)], axis=0
    )

    returned = peers_exchange(slot_grad)
    (grad_atoms,) = call(
        finish_kernel,
        [("auto", (atoms_n, features), BF16)],
        [("auto", send_rows), ("vmem", height_rows), ("vmem", returned)],
        megabytes=8,
    )

    def rows_of_lanes(value):
        return value.reshape(-1, C)

    new_params, new_one, new_two = adam_step(
        rows_of_lanes(params), rows_of_lanes(adam_m), rows_of_lanes(adam_v), grads.astype(F32)
    )
    return (
        output,
        grad_atoms,
        new_params.reshape(-1),
        new_one.reshape(-1),
        new_two.reshape(-1),
    )


def solution(mesh):
    return jax.shard_map(
        shards,
        mesh=mesh,
        in_specs=(
            P(("node", "edge"), None),
            P(("node", "edge"), None),
            P("node"),
            P("node"),
            P("node"),
            P("node", "edge", None),
            P(("node", "edge"), None),
            P(("node", "edge"), None),
            P(),
            P(("node", "edge"), None),
            P("node", "edge"),
        ),
        out_specs=(
            P(("node", "edge"), None),
            P(("node", "edge"), None),
            P("node"),
            P("node"),
            P("node"),
        ),
        check_vma=False,
    )
```

```python
import functools

import jax
import jax.numpy as jnp
from jax import lax
from jax.experimental import pallas as pl
from jax.experimental.pallas import tpu as pltpu
from jax.sharding import PartitionSpec as P


C = 128
HARM = 9
FFH = 256
K = 4
TILE_ATOMS = 32
ROTS = 64
SUB = 8
TURN_ROWS = 88
GROUPS = 4

harmonic_order = (0, 2, 6, 3, 7, 1, 5, 8, 4)
norm_epsilon = 1e-06
first_beta = 0.8
second_beta = 0.95
step_count = 100
learn_rate = 0.01
decay_rate = 0.01
adam_epsilon = 1e-08
grad_boost = 4.0

F32 = jnp.float32
BF16 = jnp.bfloat16

degree_block = (0, 1, 1, 1, 2, 2, 2, 2, 2)
entries = [
    (row, col, harmonic_order[row] * HARM + col)
    for row in range(HARM)
    for col in range(HARM)
    if degree_block[harmonic_order[row]] == degree_block[col]
]
cols_of = [[col for r, col, _ in entries if r == row] for row in range(HARM)]
rows_of = [[row for row, c, _ in entries if c == col] for col in range(HARM)]

ZERO, ONE, TWO = 3 * C, 4 * C, 2 * C
row_scale = [ZERO**-0.5] * 3 + [ONE**-0.5] * 4 + [TWO**-0.5] * 2
piece_rows = [9 * C, 4 * C, 4 * C, C, C, 2 * C, 2 * C, 2 * C]
piece_start = [sum(piece_rows[:i]) for i in range(len(piece_rows))]
PACK_ROWS = sum(piece_rows)


def lanes(number, width=C):
    return slice(number * width, (number + 1) * width)


def dot(left, right, left_dim=1, right_dim=0):
    return lax.dot_general(
        left, right, (((left_dim,), (right_dim,)), ((), ())), preferred_element_type=F32
    )


def split_parts(value, count):
    parts = []
    for _ in range(count):
        part = value.astype(BF16)
        parts.append(part)
        value = value - part.astype(F32)
    return parts


def as_low(mask):
    return jnp.where(mask, 1.0, 0.0).astype(BF16)


def pick_kernel(sends_ref, atoms_ref, params_ref, rows_ref, own_ref):
    shape = (atoms_ref.shape[0], sends_ref.shape[1])
    picks = as_low(lax.broadcasted_iota(jnp.int32, shape, 0) == sends_ref[...])
    rows_ref[...] = dot(picks, atoms_ref[...], 0, 0).astype(BF16)
    own_ref[...] = params_ref[...].astype(BF16)


def arrange_kernel(live_ref, atoms_ref, cot_ref, index_ref, gain_ref, table_ref, *outs):
    atoms_t_ref, cot_t_ref, turn_ref, gain_out_ref = outs
    atoms_n = atoms_ref.shape[0]
    is_live = lax.broadcasted_iota(jnp.int32, (K, atoms_n), 1) < live_ref[0, 0] * TILE_ATOMS
    gain_out_ref[...] = jnp.where(is_live, gain_ref[...], 0.0) * K**-0.5
    for col in range(HARM):
        atoms_t_ref[:, lanes(col, atoms_n)] = atoms_ref[:, lanes(col)].T
        cot_t_ref[:, lanes(col, atoms_n)] = cot_ref[:, lanes(col)].T
    pieces = split_parts(table_ref[...], 3)
    range_of_table = lax.broadcasted_iota(jnp.int32, (ROTS, atoms_n), 0)
    for k in range(K):
        chosen = as_low(range_of_table == index_ref[k : k + 1, :])
        turn_ref[pl.ds(k * TURN_ROWS, HARM * HARM), :] = sum(dot(piece, chosen) for piece in pieces)


def unpack_kernel(node_count, *refs):
    shard_refs = refs[:node_count]
    out_refs = refs[node_count : node_count + 12]
    built = refs[node_count + 12 : node_count + 24]
    packed, arrived = refs[node_count + 24 :]
    (
        zero_ref,
        one_ref,
        two_ref,
        zero_t_ref,
        one_t_ref,
        two_t_ref,
        gate_ref,
        up_ref,
        down_ref,
        gate_t_ref,
        up_t_ref,
        down_t_ref,
    ) = built
    copies = [
        pltpu.make_async_copy(source, target, arrived.at[number])
        for number, (source, target) in enumerate(zip(built, out_refs))
    ]
    node = lax.axis_index("node")

    shard_rows = PACK_ROWS // node_count
    for distance in range(node_count):
        first = pl.multiple_of((node ^ distance) * shard_rows, 8)
        packed[pl.ds(first, shard_rows), :] = shard_refs[distance][...].astype(F32)

    def unpack(piece, rows, width, *targets):
        for part in range(width):
            first = piece_start[piece] + part
            block = packed[pl.ds(first, rows, stride=width), :].astype(BF16)
            turned_block = block.T
            for target, turned, row, col, sign in targets:
                value = turned_block if turned else block
                value = value if sign > 0 else -value
                if turned:
                    target[col + part * C : col + (part + 1) * C, row : row + rows] = value
                else:
                    target[row : row + rows, col + part * C : col + (part + 1) * C] = value

    half = 2 * C
    unpack(0, ZERO, 3, (zero_t_ref, True, 0, 0, 1), (zero_ref, False, 0, 0, 1))
    copies[3].start()
    copies[0].start()
    for piece, matrix, turned, rows, places in (
        (1, one_ref, one_t_ref, half, (1, 4)),
        (3, two_ref, two_t_ref, C, (2, 5)),
    ):
        width = rows // C
        unpack(
            piece,
            rows,
            width,
            (turned, True, 0, 0, 1),
            (turned, True, rows, rows, 1),
            (matrix, False, 0, 0, 1),
            (matrix, False, rows, rows, 1),
        )
        unpack(
            piece + 1,
            rows,
            width,
            (turned, True, 0, rows, 1),
            (turned, True, rows, 0, -1),
            (matrix, False, 0, rows, 1),
            (matrix, False, rows, 0, -1),
        )
        for place in places:
            copies[place].start()
    unpack(5, C, 2, (gate_ref, False, 0, 0, 1), (gate_t_ref, True, 0, 0, 1))
    unpack(6, C, 2, (up_ref, False, 0, 0, 1), (up_t_ref, True, 0, 0, 1))
    unpack(7, FFH, 1, (down_ref, False, 0, 0, 1), (down_t_ref, True, 0, 0, 1))
    for copy in copies[6:]:
        copy.start()
    for copy in copies:
        copy.wait()


def turns_of(turn_ref, k, factors=None):
    values = {}
    for row, col, entry in entries:
        value = turn_ref[pl.ds(k * TURN_ROWS + entry, SUB, stride=0), :]
        values[row, col] = value if factors is None else value * factors[row]
    return values


def over_channels(body):
    def step(number, carry):
        for part in range(GROUPS):
            body(pl.multiple_of((number * GROUPS + part) * 2 * SUB, 2 * SUB))
        return carry

    lax.fori_loop(0, C // (2 * SUB * GROUPS), step, 0)


def flat(value):
    return value.reshape(value.shape[0] * value.shape[1], value.shape[2])


ZERO_PART, ONE_PART, TWO_PART = slice(0, 3), slice(3, 7), slice(7, 9)


def main_kernel(edge_parts, node_count, all_atoms, *refs):
    rows_ref = refs[0]
    sides = refs[1:15]
    output_ref, height_grad, grad_mixed, keep_ref, send_ref = refs[15:20]
    held = refs[20:34]
    slot_ref, turn, gain_ref = held[:3]
    (zero_t, one_t, two_t, gate_w, up_w, down_w, gate_t, up_t, down_t, atoms_t, cot_t) = held[3:]
    (
        output_rows,
        arrived,
        source,
        rotated,
        mixed,
        height,
        normed_low,
        up_value,
        hidden,
        grad_up,
        packed,
    ) = refs[34:]
    copies = [
        pltpu.make_async_copy(side, target, arrived.at[number])
        for number, (side, target) in enumerate(zip(sides, held))
    ]
    early, late = copies[:3], copies[3:]
    for copy in early + late:
        copy.start()
    output_copy = pltpu.make_async_copy(output_rows, output_ref, arrived.at[len(copies)])
    atoms_n = output_ref.shape[0]
    slots_n = rows_ref.shape[0]
    node = lax.axis_index("node")

    slot_range = lax.broadcasted_iota(jnp.int32, (slots_n, atoms_n), 0)
    for copy in early:
        copy.wait()
    taken = jnp.concatenate(
        [as_low(slot_range == slot_ref[k : k + 1, :]) for k in range(K)], axis=1
    )
    source[...] = dot(rows_ref[...], taken, 0, 0).reshape(source.shape)
    gains = gain_ref[...]

    for k in range(K):
        here = lanes(k, atoms_n)
        turns = turns_of(turn, k)

        def rotate(first, here=here, turns=turns):
            halves = []
            for start in (0, SUB):
                values = [source[col, pl.ds(first + start, SUB), here] for col in range(HARM)]
                halves.append(
                    [
                        sum(turns[row, col] * values[col] for col in cols_of[row])
                        for row in range(HARM)
                    ]
                )
            for row in range(HARM):
                pair = jnp.concatenate([halves[0][row], halves[1][row]], axis=0)
                rotated[row, pl.ds(first, 2 * SUB), here] = pair.astype(BF16)

        over_channels(rotate)
    for copy in late:
        copy.wait()
    for part, matrix in ((ZERO_PART, zero_t), (ONE_PART, one_t), (TWO_PART, two_t)):
        mixed[part] = dot(matrix[...], flat(rotated[part])).reshape(mixed[part].shape)

    for k in range(K):
        here = lanes(k, atoms_n)
        gain = jnp.broadcast_to(gains[k : k + 1, :], (SUB, atoms_n))
        turns = turns_of(turn, k, [gain * scale for scale in row_scale])

        def gather_messages(first, k=k, here=here, turns=turns):
            if k == 0:
                starts = [
                    atoms_t[pl.ds(first, 2 * SUB), lanes(col, atoms_n)].astype(F32)
                    for col in range(HARM)
                ]
            for start in (0, SUB):
                values = [mixed[row, pl.ds(first + start, SUB), here] for row in range(HARM)]
                target = pl.ds(first + start, SUB)
                for col in range(HARM):
                    there = lanes(col, atoms_n)
                    base = starts[col][start : start + SUB] if k == 0 else height[target, there]
                    total = sum(turns[row, col] * values[row] for row in rows_of[col])
                    height[target, there] = base + total

        over_channels(gather_messages)

    def atom_sum(value):
        total = sum(value[:, lanes(col, atoms_n)] for col in range(HARM))
        return jnp.sum(total, axis=0, keepdims=True)

    def each(value):
        return jnp.concatenate([value] * HARM, axis=1)

    mean = atom_sum(height[...] * height[...]) * (1.0 / (HARM * C))
    inverse = lax.rsqrt(mean + norm_epsilon)
    normed_low[...] = (height[...] * each(inverse)).astype(BF16)
    gate = jax.nn.sigmoid(dot(gate_t[...], normed_low[:, 0:atoms_n]) * C**-0.5)
    up_gate, down_gate = gate * C**-0.5, gate * FFH**-0.5
    up_value[...] = dot(up_t[...], normed_low[...])
    for col in range(HARM):
        here = lanes(col, atoms_n)
        hidden[:, here] = (up_value[:, here] * up_gate).astype(BF16)
    projected = dot(down_t[...], hidden[...])
    for col in range(HARM):
        here = lanes(col, atoms_n)
        result = (height[:, here] + projected[:, here] * FFH**-0.5).astype(BF16)
        output_rows[:, lanes(col)] = result.T
    output_copy.start()
    gate_sum = jnp.zeros_like(gate)
    for col in range(HARM):
        here = lanes(col, atoms_n)
        grad_hidden = dot(down_w[...], cot_t[:, here])
        grad_up[:, here] = (grad_hidden * down_gate).astype(BF16)
        gate_sum = gate_sum + grad_hidden * up_value[:, here]
    gate_sum = gate_sum * (C**-0.5 * FFH**-0.5)
    grad_gate = (gate_sum * gate * (1.0 - gate)).astype(BF16)
    along = dot(up_w[...], grad_up[...]) * C**-0.5
    gate_along = dot(gate_w[...], grad_gate) * C**-0.5
    along = jnp.concatenate([along[:, 0:atoms_n] + gate_along, along[:, atoms_n:]], axis=1)
    overlap = atom_sum(along * height[...]) * (inverse * (1.0 / (HARM * C)))
    height_grad[...] = cot_t[...].astype(F32) + each(inverse) * (
        along - height[...] * each(inverse * overlap)
    )

    for k in range(K):
        here = lanes(k, atoms_n)
        gain = jnp.broadcast_to(gains[k : k + 1, :], (SUB, atoms_n))
        turns = turns_of(turn, k, [gain] * HARM)

        def rotate_grads(first, here=here, turns=turns):
            halves = []
            for start in (0, SUB):
                target = pl.ds(first + start, SUB)
                values = [height_grad[target, lanes(col, atoms_n)] for col in range(HARM)]
                halves.append(
                    [
                        sum(turns[row, col] * values[col] for col in cols_of[row])
                        for row in range(HARM)
                    ]
                )
            for row in range(HARM):
                pair = jnp.concatenate([halves[0][row], halves[1][row]], axis=0)
                grad_mixed[row, pl.ds(first, 2 * SUB), here] = pair.astype(BF16)

        over_channels(rotate_grads)
    boost = grad_boost * all_atoms**-0.5

    def pack_piece(piece, rows, width, value):
        for part in range(width):
            packed[pl.ds(piece_start[piece] + part, rows, stride=width), :] = value[:, lanes(part)]

    def weight_grad(left, right, scale):
        return dot(left, right, 1, 1) * (scale * boost)

    zero_grad = weight_grad(flat(rotated[ZERO_PART]), flat(grad_mixed[ZERO_PART]), row_scale[0])
    pack_piece(0, ZERO, 3, zero_grad)
    one_grad = weight_grad(flat(rotated[ONE_PART]), flat(grad_mixed[ONE_PART]), row_scale[3])
    half = 2 * C
    pack_piece(1, half, 2, one_grad[:half, :half] + one_grad[half:, half:])
    pack_piece(2, half, 2, one_grad[:half, half:] - one_grad[half:, :half])
    two_grad = weight_grad(flat(rotated[TWO_PART]), flat(grad_mixed[TWO_PART]), row_scale[7])
    pack_piece(3, C, 1, two_grad[:C, :C] + two_grad[C:, C:])
    pack_piece(4, C, 1, two_grad[:C, C:] - two_grad[C:, :C])
    pack_piece(5, C, 2, weight_grad(normed_low[:, 0:atoms_n], grad_gate, C**-0.5))
    pack_piece(6, C, 2, weight_grad(normed_low[...], grad_up[...], C**-0.5))
    pack_piece(7, FFH, 1, weight_grad(hidden[...], cot_t[...], FFH**-0.5))
    shard_rows = PACK_ROWS // node_count
    part_rows = shard_rows // edge_parts
    edge_low = lax.axis_index("edge") & (edge_parts - 1)
    bits = node_count.bit_length() - 1
    blocks = []
    for place in range(node_count):
        distance = int(format(place, "b").zfill(bits)[::-1], 2) if bits else 0
        for part in range(edge_parts):
            blocks.append((node ^ distance) * shard_rows + (edge_low ^ part) * part_rows)
    half = len(blocks) // 2
    for number, first in enumerate(blocks):
        values = packed[pl.ds(pl.multiple_of(first, 8), part_rows), :].astype(BF16)
        target = keep_ref if number < half else send_ref
        target[lanes(number % half, part_rows), :] = values
    output_copy.wait()


def slot_kernel(grad_mixed, height_grad, *refs):
    sides, held = refs[:5], refs[7:12]
    slot_rows, height_rows_ref = refs[5:7]
    zero_w, one_w, two_w, turn, slot_ref = held
    mixed, source_high, source_low, arrived = refs[12:]
    copies = [
        pltpu.make_async_copy(side, target, arrived.at[number])
        for number, (side, target) in enumerate(zip(sides, held))
    ]
    for copy in copies:
        copy.start()
    slots_n = slot_rows.shape[0]
    atoms_n = slot_ref.shape[1]
    for col in range(HARM):
        height_rows_ref[:, lanes(col)] = height_grad[:, lanes(col, atoms_n)].T
    parts = ((ZERO_PART, zero_w), (ONE_PART, one_w), (TWO_PART, two_w))
    for (part, matrix), copy in zip(parts, copies):
        copy.wait()
        mixed[part] = dot(matrix[...], flat(grad_mixed[part])).reshape(mixed[part].shape)
    for copy in copies[3:]:
        copy.wait()
    for k in range(K):
        here = lanes(k, atoms_n)
        turns = turns_of(turn, k, row_scale)

        def rotate_back(first, here=here, turns=turns):
            halves = []
            for start in (0, SUB):
                values = [mixed[row, pl.ds(first + start, SUB), here] for row in range(HARM)]
                halves.append(
                    [
                        sum(turns[row, col] * values[row] for row in rows_of[col])
                        for col in range(HARM)
                    ]
                )
            for col in range(HARM):
                pair = jnp.concatenate([halves[0][col], halves[1][col]], axis=0)
                for target, part in zip((source_high, source_low), split_parts(pair, 2)):
                    target[col, pl.ds(first, 2 * SUB), here] = part

        over_channels(rotate_back)
    slot_range = lax.broadcasted_iota(jnp.int32, (slots_n, atoms_n), 0)
    taken = jnp.concatenate(
        [as_low(slot_range == slot_ref[k : k + 1, :]) for k in range(K)], axis=1
    )
    slot_rows[...] = dot(taken, flat(source_high[...]), 1, 1) + dot(
        taken, flat(source_low[...]), 1, 1
    )


def finish_kernel(sends_ref, height_rows_ref, back_ref, grad_ref):
    shape = (grad_ref.shape[0], sends_ref.shape[1])
    picks = as_low(lax.broadcasted_iota(jnp.int32, shape, 0) == sends_ref[...])
    pieces = split_parts(back_ref[...], 3)
    total = sum(dot(picks, piece) for piece in pieces)
    grad_ref[...] = (height_rows_ref[...] + total).astype(BF16)


def adam_step(params, moment_one, moment_two, gradient):
    new_one = first_beta * moment_one + (1.0 - first_beta) * gradient
    new_two = second_beta * moment_two + (1.0 - second_beta) * gradient * gradient
    corrected = (
        new_one
        / (1.0 - first_beta**step_count)
        / (jnp.sqrt(new_two / (1.0 - second_beta**step_count)) + adam_epsilon)
    )
    return (params - learn_rate * (corrected + decay_rate * params), new_one, new_two)


def swap(value, axis, bit):
    size = lax.axis_size(axis)
    return lax.ppermute(value, axis, [(i, i ^ (1 << bit)) for i in range(size)])


def swap_both(value, node_step, edge_step):
    nodes, edges = lax.axis_size("node"), lax.axis_size("edge")
    pairs = [
        (n * edges + e, (n ^ node_step) * edges + (e ^ edge_step))
        for n in range(nodes)
        for e in range(edges)
    ]
    return lax.ppermute(value, ("node", "edge"), pairs)


def shards(
    atoms,
    cotangent,
    params,
    adam_m,
    adam_v,
    sends,
    edge_slot,
    rot_index,
    rot_table,
    edge_gain,
    live_tiles,
):
    node_size = lax.axis_size("node")
    edge_size = lax.axis_size("edge")
    node_bits = node_size.bit_length() - 1
    edge_bits = edge_size.bit_length() - 1
    atoms_n, features = atoms.shape
    slots_n = sends.shape[-1]
    per_peer = slots_n // edge_size
    edges_n = atoms_n * K
    edge_parts = 2

    spaces = {"vmem": pltpu.VMEM, "smem": pltpu.SMEM, "hbm": pltpu.HBM, "auto": pltpu.VMEM}

    def call(kernel, outs, ins, scratch=(), megabytes=None):
        def typed_out(place, shape, dtype):
            if place in ("vmem", "hbm"):
                return spaces[place](shape, dtype)
            return jax.ShapeDtypeStruct(shape, dtype)

        def typed_in(place, value):
            if place in ("vmem", "hbm"):
                return pltpu.with_memory_space_constraint(value, spaces[place])
            return value

        limit = None if megabytes is None else megabytes << 20
        return pl.pallas_call(
            kernel,
            out_shape=tuple(typed_out(*out) for out in outs),
            in_specs=[pl.BlockSpec(memory_space=spaces[place]) for place, _ in ins],
            out_specs=tuple(pl.BlockSpec(memory_space=spaces[out[0]]) for out in outs),
            scratch_shapes=list(scratch),
            compiler_params=pltpu.CompilerParams(vmem_limit_bytes=limit),
        )(*(typed_in(*each_in) for each_in in ins))

    def peers_exchange(value):
        value = value.reshape(edge_size, per_peer, features)
        value = lax.all_to_all(value, "edge", split_axis=0, concat_axis=0, tiled=True)
        return value.reshape(slots_n, features)

    send_rows = sends.reshape(1, slots_n)
    slots_t, index_t, gains_t = edge_slot.T, rot_index.T, edge_gain.T
    table_t = jnp.transpose(rot_table, (1, 2, 0)).reshape(HARM * HARM, ROTS)
    wide = HARM * atoms_n
    outgoing, own = call(
        pick_kernel,
        [("vmem", (slots_n, features), BF16), ("vmem", (PACK_ROWS // node_size, C), BF16)],
        [("auto", value) for value in (send_rows, atoms, params.reshape(-1, C))],
    )
    slot_rows = peers_exchange(outgoing)
    by_distance = {0: own}
    for bit in reversed(range(node_bits)):
        for distance in list(by_distance):
            by_distance[distance | (1 << bit)] = swap(by_distance[distance], "node", bit)
    matrix_shapes = [(ZERO, ZERO), (ONE, ONE), (TWO, TWO)]
    unpacked_shapes = matrix_shapes * 2 + [(C, FFH)] * 2 + [(FFH, C)] * 3 + [(C, FFH)]
    atoms_t, cot_t, turn, gains_kept = call(
        arrange_kernel,
        [
            ("auto", (C, wide), BF16),
            ("auto", (C, wide), BF16),
            ("auto", (K * TURN_ROWS, atoms_n), F32),
            ("auto", (K, atoms_n), F32),
        ],
        [("smem", live_tiles)]
        + [("auto", value) for value in (atoms, cotangent, index_t, gains_t, table_t)],
    )
    unpacked = call(
        functools.partial(unpack_kernel, node_size),
        [("hbm", shape, BF16) for shape in unpacked_shapes],
        [("vmem", by_distance[distance]) for distance in range(node_size)],
        [
            *(pltpu.VMEM(shape, BF16) for shape in unpacked_shapes),
            pltpu.VMEM((PACK_ROWS, C), F32),
            pltpu.SemaphoreType.DMA((len(unpacked_shapes),)),
        ],
        megabytes=16,
    )
    sides = (slots_t, turn, gains_kept, *unpacked[3:], atoms_t, cot_t)
    read_again = (*unpacked[:3], turn, slots_t)
    output, height_grad, grad_mixed, keep, send = call(
        functools.partial(main_kernel, edge_parts, node_size, atoms_n * node_size * edge_size),
        [
            ("hbm", (atoms_n, features), BF16),
            ("vmem", (C, wide), F32),
            ("vmem", (HARM, C, edges_n), BF16),
            ("vmem", (PACK_ROWS // 2, C), BF16),
            ("vmem", (PACK_ROWS // 2, C), BF16),
        ],
        [("vmem", slot_rows)]
        + [("hbm", value) for value in sides],
        [
            *(pltpu.VMEM(value.shape, value.dtype) for value in sides),
            pltpu.VMEM((atoms_n, features), BF16),
            pltpu.SemaphoreType.DMA((len(sides) + 1,)),
            pltpu.VMEM((HARM, C, edges_n), F32),
            pltpu.VMEM((HARM, C, edges_n), BF16),
            pltpu.VMEM((HARM, C, edges_n), F32),
            pltpu.VMEM((C, wide), F32),
            pltpu.VMEM((C, wide), BF16),
            pltpu.VMEM((FFH, wide), F32),
            pltpu.VMEM((FFH, wide), BF16),
            pltpu.VMEM((FFH, wide), BF16),
            pltpu.VMEM((PACK_ROWS, C), F32),
        ],
        megabytes=28,
    )
    slot_grad, height_rows = call(
        slot_kernel,
        [("vmem", (slots_n, features), F32), ("vmem", (atoms_n, features), F32)],
        [("vmem", grad_mixed), ("vmem", height_grad)]
        + [("hbm", value) for value in read_again],
        [
            *(pltpu.VMEM(value.shape, value.dtype) for value in read_again),
            pltpu.VMEM((HARM, C, edges_n), F32),
            pltpu.VMEM((HARM, C, edges_n), BF16),
            pltpu.VMEM((HARM, C, edges_n), BF16),
            pltpu.SemaphoreType.DMA((len(read_again),)),
        ],
        megabytes=20,
    )

    def add_low(left, right):
        return (left.astype(F32) + right.astype(F32)).astype(BF16)

    for bit in range(node_bits - 1):
        if bit:
            half = keep.shape[0] // 2
            keep, send = keep[:half], keep[half:]
        keep = add_low(keep, swap(send, "node", bit))
    quarter = keep.shape[0] // 4
    total = keep[:quarter].astype(F32)
    for number in (2, 3, 1):
        came = swap_both(
            keep[number * quarter : (number + 1) * quarter],
            (number >> 1) << (node_bits - 1),
            number & 1,
        )
        total = total + came.astype(F32)
    grads = total.astype(BF16)
    for bit in reversed(range(2, edge_bits)):
        grads = add_low(grads, swap(grads, "edge", bit))
    far = swap_both(grads, 0, 2)
    both = swap_both(grads, 0, 3)
    near = swap_both(grads, 0, 1)
    own_half = grads.astype(F32) + far.astype(F32)
    other_half = near.astype(F32) + both.astype(F32)
    is_low = (lax.axis_index("edge") & 1) == 0
    grads = jnp.concatenate(
        [jnp.where(is_low, own_half, other_half), jnp.where(is_low, other_half, own_half)],
        axis=0,
    )

    returned = peers_exchange(slot_grad)
    (grad_atoms,) = call(
        finish_kernel,
        [("auto", (atoms_n, features), BF16)],
        [("auto", send_rows), ("vmem", height_rows), ("vmem", returned)],
        megabytes=8,
    )

    def rows_of_lanes(value):
        return value.reshape(-1, C)

    new_params, new_one, new_two = adam_step(
        rows_of_lanes(params), rows_of_lanes(adam_m), rows_of_lanes(adam_v), grads
    )
    return (
        output,
        grad_atoms,
        new_params.reshape(-1),
        new_one.reshape(-1),
        new_two.reshape(-1),
    )


def solution(mesh):
    return jax.shard_map(
        shards,
        mesh=mesh,
        in_specs=(
            P(("node", "edge"), None),
            P(("node", "edge"), None),
            P("node"),
            P("node"),
            P("node"),
            P("node", "edge", None),
            P(("node", "edge"), None),
            P(("node", "edge"), None),
            P(),
            P(("node", "edge"), None),
            P("node", "edge"),
        ),
        out_specs=(
            P(("node", "edge"), None),
            P(("node", "edge"), None),
            P("node"),
            P("node"),
            P("node"),
        ),
        check_vma=False,
    )
```

```python
import functools

import jax
import jax.numpy as jnp
from jax import lax
from jax.experimental import pallas as pl
from jax.experimental.pallas import tpu as pltpu
from jax.sharding import PartitionSpec as P


C = 128
HARM = 9
FFH = 256
K = 4
TILE_ATOMS = 32
ROTS = 64
SUB = 8
TURN_ROWS = 88
GROUPS = 4
CHUNK = 4

harmonic_order = (0, 2, 6, 3, 7, 1, 5, 8, 4)
norm_epsilon = 1e-06
first_beta = 0.8
second_beta = 0.95
step_count = 100
learn_rate = 0.01
decay_rate = 0.01
adam_epsilon = 1e-08
grad_boost = 4.0

F32 = jnp.float32
BF16 = jnp.bfloat16

degree_block = (0, 1, 1, 1, 2, 2, 2, 2, 2)
entries = [
    (row, col, harmonic_order[row] * HARM + col)
    for row in range(HARM)
    for col in range(HARM)
    if degree_block[harmonic_order[row]] == degree_block[col]
]
cols_of = [[col for r, col, _ in entries if r == row] for row in range(HARM)]
rows_of = [[row for row, c, _ in entries if c == col] for col in range(HARM)]

ZERO, ONE, TWO = 3 * C, 4 * C, 2 * C
row_scale = [ZERO**-0.5] * 3 + [ONE**-0.5] * 4 + [TWO**-0.5] * 2
piece_rows = [9 * C, 4 * C, 4 * C, C, C, 2 * C, 2 * C, 2 * C]
piece_start = [sum(piece_rows[:i]) for i in range(len(piece_rows))]
PACK_ROWS = sum(piece_rows)


def lanes(number, width=C):
    return slice(number * width, (number + 1) * width)


def dot(left, right, left_dim=1, right_dim=0):
    return lax.dot_general(
        left, right, (((left_dim,), (right_dim,)), ((), ())), preferred_element_type=F32
    )


def split_parts(value, count):
    parts = []
    for _ in range(count):
        part = value.astype(BF16)
        parts.append(part)
        value = value - part.astype(F32)
    return parts


def as_low(mask):
    return jnp.where(mask, 1.0, 0.0).astype(BF16)


def pick_kernel(sends_ref, atoms_ref, params_ref, rows_ref, own_ref):
    shape = (atoms_ref.shape[0], sends_ref.shape[1])
    picks = as_low(lax.broadcasted_iota(jnp.int32, shape, 0) == sends_ref[...])
    rows_ref[...] = dot(picks, atoms_ref[...], 0, 0).astype(BF16)
    own_ref[...] = params_ref[...].astype(BF16)


def arrange_kernel(live_ref, atoms_ref, cot_ref, index_ref, gain_ref, table_ref, *outs):
    atoms_t_ref, cot_t_ref, turn_ref, gain_out_ref = outs
    atoms_n = atoms_ref.shape[0]
    is_live = lax.broadcasted_iota(jnp.int32, (K, atoms_n), 1) < live_ref[0, 0] * TILE_ATOMS
    gain_out_ref[...] = jnp.where(is_live, gain_ref[...], 0.0) * K**-0.5
    for col in range(HARM):
        atoms_t_ref[:, lanes(col, atoms_n)] = atoms_ref[:, lanes(col)].T
        cot_t_ref[:, lanes(col, atoms_n)] = cot_ref[:, lanes(col)].T
    pieces = split_parts(table_ref[...], 3)
    range_of_table = lax.broadcasted_iota(jnp.int32, (ROTS, atoms_n), 0)
    for k in range(K):
        chosen = as_low(range_of_table == index_ref[k : k + 1, :])
        turn_ref[pl.ds(k * TURN_ROWS, HARM * HARM), :] = sum(dot(piece, chosen) for piece in pieces)


def unpack_kernel(node_count, *refs):
    shard_refs = refs[:node_count]
    out_refs = refs[node_count : node_count + 12]
    built = refs[node_count + 12 : node_count + 24]
    packed, arrived = refs[node_count + 24 :]
    (
        zero_ref,
        one_ref,
        two_ref,
        zero_t_ref,
        one_t_ref,
        two_t_ref,
        gate_ref,
        up_ref,
        down_ref,
        gate_t_ref,
        up_t_ref,
        down_t_ref,
    ) = built
    copies = [
        pltpu.make_async_copy(source, target, arrived.at[number])
        for number, (source, target) in enumerate(zip(built, out_refs))
    ]
    node = lax.axis_index("node")

    shard_rows = PACK_ROWS // node_count
    for distance in range(node_count):
        first = pl.multiple_of((node ^ distance) * shard_rows, 8)
        packed[pl.ds(first, shard_rows), :] = shard_refs[distance][...].astype(F32)

    def unpack(piece, rows, width, *targets):
        for part in range(width):
            first = piece_start[piece] + part
            block = packed[pl.ds(first, rows, stride=width), :].astype(BF16)
            turned_block = block.T
            for target, turned, row, col, sign in targets:
                value = turned_block if turned else block
                value = value if sign > 0 else -value
                if turned:
                    target[col + part * C : col + (part + 1) * C, row : row + rows] = value
                else:
                    target[row : row + rows, col + part * C : col + (part + 1) * C] = value

    half = 2 * C
    unpack(0, ZERO, 3, (zero_t_ref, True, 0, 0, 1), (zero_ref, False, 0, 0, 1))
    copies[3].start()
    copies[0].start()
    for piece, matrix, turned, rows, places in (
        (1, one_ref, one_t_ref, half, (1, 4)),
        (3, two_ref, two_t_ref, C, (2, 5)),
    ):
        width = rows // C
        unpack(
            piece,
            rows,
            width,
            (turned, True, 0, 0, 1),
            (turned, True, rows, rows, 1),
            (matrix, False, 0, 0, 1),
            (matrix, False, rows, rows, 1),
        )
        unpack(
            piece + 1,
            rows,
            width,
            (turned, True, 0, rows, 1),
            (turned, True, rows, 0, -1),
            (matrix, False, 0, rows, 1),
            (matrix, False, rows, 0, -1),
        )
        for place in places:
            copies[place].start()
    unpack(5, C, 2, (gate_ref, False, 0, 0, 1), (gate_t_ref, True, 0, 0, 1))
    unpack(6, C, 2, (up_ref, False, 0, 0, 1), (up_t_ref, True, 0, 0, 1))
    unpack(7, FFH, 1, (down_ref, False, 0, 0, 1), (down_t_ref, True, 0, 0, 1))
    for copy in copies[6:]:
        copy.start()
    for copy in copies:
        copy.wait()


def turns_of(turn_ref, k, factors=None):
    values = {}
    for row, col, entry in entries:
        value = turn_ref[pl.ds(k * TURN_ROWS + entry, SUB, stride=0), :]
        values[row, col] = value if factors is None else value * factors[row]
    return values


def over_channels(body):
    def step(number, carry):
        for part in range(GROUPS):
            body(pl.multiple_of((number * GROUPS + part) * 2 * SUB, 2 * SUB))
        return carry

    lax.fori_loop(0, C // (2 * SUB * GROUPS), step, 0)


def flat(value):
    return value.reshape(value.shape[0] * value.shape[1], value.shape[2])


ZERO_PART, ONE_PART, TWO_PART = slice(0, 3), slice(3, 7), slice(7, 9)


def main_kernel(edge_parts, node_count, all_atoms, *refs):
    rows_ref = refs[0]
    sides = refs[1:15]
    output_ref, height_grad, grad_mixed, keep_ref, send_ref = refs[15:20]
    held = refs[20:34]
    slot_ref, turn, gain_ref = held[:3]
    (zero_t, one_t, two_t, gate_w, up_w, down_w, gate_t, up_t, down_t, atoms_t, cot_t) = held[3:]
    (
        output_rows,
        arrived,
        source,
        rotated,
        mixed,
        height,
        normed_low,
        hidden,
        grad_up,
        packed,
    ) = refs[34:]
    copies = [
        pltpu.make_async_copy(side, target, arrived.at[number])
        for number, (side, target) in enumerate(zip(sides, held))
    ]
    early, late = copies[:3], copies[3:]
    for copy in early + late:
        copy.start()
    output_copy = pltpu.make_async_copy(output_rows, output_ref, arrived.at[len(copies)])
    atoms_n = output_ref.shape[0]
    slots_n = rows_ref.shape[0]
    node = lax.axis_index("node")

    slot_range = lax.broadcasted_iota(jnp.int32, (slots_n, atoms_n), 0)
    for copy in early:
        copy.wait()
    taken = jnp.concatenate(
        [as_low(slot_range == slot_ref[k : k + 1, :]) for k in range(K)], axis=1
    )
    source[...] = dot(rows_ref[...], taken, 0, 0).reshape(source.shape)
    gains = gain_ref[...]

    for k in range(K):
        here = lanes(k, atoms_n)
        turns = turns_of(turn, k)

        def rotate(first, here=here, turns=turns):
            halves = []
            for start in (0, SUB):
                values = [source[col, pl.ds(first + start, SUB), here] for col in range(HARM)]
                halves.append(
                    [
                        sum(turns[row, col] * values[col] for col in cols_of[row])
                        for row in range(HARM)
                    ]
                )
            for row in range(HARM):
                pair = jnp.concatenate([halves[0][row], halves[1][row]], axis=0)
                rotated[row, pl.ds(first, 2 * SUB), here] = pair.astype(BF16)

        over_channels(rotate)
    for copy in late:
        copy.wait()
    for part, matrix in ((ZERO_PART, zero_t), (ONE_PART, one_t), (TWO_PART, two_t)):
        mixed[part] = dot(matrix[...], flat(rotated[part])).reshape(mixed[part].shape)

    for k in range(K):
        here = lanes(k, atoms_n)
        gain = jnp.broadcast_to(gains[k : k + 1, :], (SUB, atoms_n))
        turns = turns_of(turn, k, [gain * scale for scale in row_scale])

        def gather_messages(first, k=k, here=here, turns=turns):
            if k == 0:
                starts = [
                    atoms_t[pl.ds(first, 2 * SUB), lanes(col, atoms_n)].astype(F32)
                    for col in range(HARM)
                ]
            for start in (0, SUB):
                values = [mixed[row, pl.ds(first + start, SUB), here] for row in range(HARM)]
                target = pl.ds(first + start, SUB)
                for col in range(HARM):
                    there = lanes(col, atoms_n)
                    base = starts[col][start : start + SUB] if k == 0 else height[target, there]
                    total = sum(turns[row, col] * values[row] for row in rows_of[col])
                    height[target, there] = base + total

        over_channels(gather_messages)

    squares = jnp.zeros((C, atoms_n), F32)
    for col in range(HARM):
        value = height[:, lanes(col, atoms_n)]
        squares = squares + value * value
    mean = jnp.sum(squares, axis=0, keepdims=True) * (1.0 / (HARM * C))
    inverse = jnp.broadcast_to(lax.rsqrt(mean + norm_epsilon), (C, atoms_n))
    for col in range(HARM):
        here = lanes(col, atoms_n)
        normed_low[:, here] = (height[:, here] * inverse).astype(BF16)
    gate = jax.nn.sigmoid(dot(gate_t[...], normed_low[:, 0:atoms_n]) * C**-0.5)
    up_gate, down_gate = gate * C**-0.5, gate * FFH**-0.5
    chunks = [list(range(col, min(col + CHUNK, HARM))) for col in range(0, HARM, CHUNK)]
    gate_sum = jnp.zeros_like(gate)
    for chunk in chunks:
        wide = slice(chunk[0] * atoms_n, (chunk[-1] + 1) * atoms_n)
        up_here = dot(up_t[...], normed_low[:, wide])
        grad_here = dot(down_w[...], cot_t[:, wide])
        for place, col in enumerate(chunk):
            here, there = lanes(col, atoms_n), lanes(place, atoms_n)
            hidden[:, here] = (up_here[:, there] * up_gate).astype(BF16)
            grad_up[:, here] = (grad_here[:, there] * down_gate).astype(BF16)
            gate_sum = gate_sum + grad_here[:, there] * up_here[:, there]
    gate_sum = gate_sum * (C**-0.5 * FFH**-0.5)
    grad_gate = (gate_sum * gate * (1.0 - gate)).astype(BF16)
    overlap = jnp.zeros((C, atoms_n), F32)
    for chunk in chunks:
        wide = slice(chunk[0] * atoms_n, (chunk[-1] + 1) * atoms_n)
        projected = dot(down_t[...], hidden[:, wide])
        along = dot(up_w[...], grad_up[:, wide])
        for place, col in enumerate(chunk):
            here, there = lanes(col, atoms_n), lanes(place, atoms_n)
            value = height[:, here]
            output_rows[:, lanes(col)] = (
                (value + projected[:, there] * FFH**-0.5).astype(BF16).T
            )
            along_here = along[:, there]
            if col == 0:
                along_here = along_here + dot(gate_w[...], grad_gate)
            height_grad[:, here] = along_here
            overlap = overlap + along_here * value
    output_copy.start()
    overlap = jnp.sum(overlap, axis=0, keepdims=True) * (C**-0.5 / (HARM * C))
    scale = inverse * C**-0.5
    weight = inverse * inverse * (inverse * overlap)
    for col in range(HARM):
        here = lanes(col, atoms_n)
        height_grad[:, here] = (
            cot_t[:, here].astype(F32) + scale * height_grad[:, here] - weight * height[:, here]
        )

    for k in range(K):
        here = lanes(k, atoms_n)
        gain = jnp.broadcast_to(gains[k : k + 1, :], (SUB, atoms_n))
        turns = turns_of(turn, k, [gain] * HARM)

        def rotate_grads(first, here=here, turns=turns):
            halves = []
            for start in (0, SUB):
                target = pl.ds(first + start, SUB)
                values = [height_grad[target, lanes(col, atoms_n)] for col in range(HARM)]
                halves.append(
                    [
                        sum(turns[row, col] * values[col] for col in cols_of[row])
                        for row in range(HARM)
                    ]
                )
            for row in range(HARM):
                pair = jnp.concatenate([halves[0][row], halves[1][row]], axis=0)
                grad_mixed[row, pl.ds(first, 2 * SUB), here] = pair.astype(BF16)

        over_channels(rotate_grads)
    boost = grad_boost * all_atoms**-0.5

    def pack_piece(piece, rows, width, value):
        for part in range(width):
            packed[pl.ds(piece_start[piece] + part, rows, stride=width), :] = value[:, lanes(part)]

    def weight_grad(left, right, scale):
        return dot(left, right, 1, 1) * (scale * boost)

    zero_grad = weight_grad(flat(rotated[ZERO_PART]), flat(grad_mixed[ZERO_PART]), row_scale[0])
    pack_piece(0, ZERO, 3, zero_grad)
    one_grad = weight_grad(flat(rotated[ONE_PART]), flat(grad_mixed[ONE_PART]), row_scale[3])
    half = 2 * C
    pack_piece(1, half, 2, one_grad[:half, :half] + one_grad[half:, half:])
    pack_piece(2, half, 2, one_grad[:half, half:] - one_grad[half:, :half])
    two_grad = weight_grad(flat(rotated[TWO_PART]), flat(grad_mixed[TWO_PART]), row_scale[7])
    pack_piece(3, C, 1, two_grad[:C, :C] + two_grad[C:, C:])
    pack_piece(4, C, 1, two_grad[:C, C:] - two_grad[C:, :C])
    pack_piece(5, C, 2, weight_grad(normed_low[:, 0:atoms_n], grad_gate, C**-0.5))
    pack_piece(6, C, 2, weight_grad(normed_low[...], grad_up[...], C**-0.5))
    pack_piece(7, FFH, 1, weight_grad(hidden[...], cot_t[...], FFH**-0.5))
    shard_rows = PACK_ROWS // node_count
    part_rows = shard_rows // edge_parts
    edge_low = lax.axis_index("edge") & (edge_parts - 1)
    high_bits = node_count.bit_length() - 2
    blocks = []
    for low in range(2):
        for part in range(edge_parts):
            for place in range(node_count // 2):
                high = int(format(place, "b").zfill(high_bits)[::-1], 2) if high_bits else 0
                distance = low | (high << 1)
                blocks.append((node ^ distance) * shard_rows + (edge_low ^ part) * part_rows)
    half = len(blocks) // 2
    for number, first in enumerate(blocks):
        if part_rows % SUB == 0:
            first = pl.multiple_of(first, SUB)
        values = packed[pl.ds(first, part_rows), :].astype(BF16)
        target = keep_ref if number < half else send_ref
        target[lanes(number % half, part_rows), :] = values
    output_copy.wait()


def slot_kernel(grad_mixed, height_grad, *refs):
    sides, held = refs[:5], refs[7:12]
    slot_rows, height_rows_ref = refs[5:7]
    zero_w, one_w, two_w, turn, slot_ref = held
    mixed, source_high, source_low, arrived = refs[12:]
    copies = [
        pltpu.make_async_copy(side, target, arrived.at[number])
        for number, (side, target) in enumerate(zip(sides, held))
    ]
    for copy in copies:
        copy.start()
    slots_n = slot_rows.shape[0]
    atoms_n = slot_ref.shape[1]
    for col in range(HARM):
        height_rows_ref[:, lanes(col)] = height_grad[:, lanes(col, atoms_n)].T
    parts = ((ZERO_PART, zero_w), (ONE_PART, one_w), (TWO_PART, two_w))
    for (part, matrix), copy in zip(parts, copies):
        copy.wait()
        mixed[part] = dot(matrix[...], flat(grad_mixed[part])).reshape(mixed[part].shape)
    for copy in copies[3:]:
        copy.wait()
    for k in range(K):
        here = lanes(k, atoms_n)
        turns = turns_of(turn, k, row_scale)

        def rotate_back(first, here=here, turns=turns):
            halves = []
            for start in (0, SUB):
                values = [mixed[row, pl.ds(first + start, SUB), here] for row in range(HARM)]
                halves.append(
                    [
                        sum(turns[row, col] * values[row] for row in rows_of[col])
                        for col in range(HARM)
                    ]
                )
            for col in range(HARM):
                pair = jnp.concatenate([halves[0][col], halves[1][col]], axis=0)
                for target, part in zip((source_high, source_low), split_parts(pair, 2)):
                    target[col, pl.ds(first, 2 * SUB), here] = part

        over_channels(rotate_back)
    slot_range = lax.broadcasted_iota(jnp.int32, (slots_n, atoms_n), 0)
    taken = jnp.concatenate(
        [as_low(slot_range == slot_ref[k : k + 1, :]) for k in range(K)], axis=1
    )
    slot_rows[...] = dot(taken, flat(source_high[...]), 1, 1) + dot(
        taken, flat(source_low[...]), 1, 1
    )


def finish_kernel(sends_ref, height_rows_ref, back_ref, grad_ref):
    shape = (grad_ref.shape[0], sends_ref.shape[1])
    picks = as_low(lax.broadcasted_iota(jnp.int32, shape, 0) == sends_ref[...])
    pieces = split_parts(back_ref[...], 3)
    total = sum(dot(picks, piece) for piece in pieces)
    grad_ref[...] = (height_rows_ref[...] + total).astype(BF16)


def adam_step(params, moment_one, moment_two, gradient):
    new_one = first_beta * moment_one + (1.0 - first_beta) * gradient
    new_two = second_beta * moment_two + (1.0 - second_beta) * gradient * gradient
    corrected = (
        new_one
        / (1.0 - first_beta**step_count)
        / (jnp.sqrt(new_two / (1.0 - second_beta**step_count)) + adam_epsilon)
    )
    return (params - learn_rate * (corrected + decay_rate * params), new_one, new_two)


def swap(value, axis, bit):
    size = lax.axis_size(axis)
    return lax.ppermute(value, axis, [(i, i ^ (1 << bit)) for i in range(size)])


def swap_edge(value, step):
    return lax.ppermute(value, "edge", [(e, e ^ step) for e in range(lax.axis_size("edge"))])


def shards(
    atoms,
    cotangent,
    params,
    adam_m,
    adam_v,
    sends,
    edge_slot,
    rot_index,
    rot_table,
    edge_gain,
    live_tiles,
):
    node_size = lax.axis_size("node")
    edge_size = lax.axis_size("edge")
    node_bits = node_size.bit_length() - 1
    edge_bits = edge_size.bit_length() - 1
    atoms_n, features = atoms.shape
    slots_n = sends.shape[-1]
    per_peer = slots_n // edge_size
    edges_n = atoms_n * K

    spaces = {"vmem": pltpu.VMEM, "smem": pltpu.SMEM, "hbm": pltpu.HBM, "auto": pltpu.VMEM}

    def call(kernel, outs, ins, scratch=(), megabytes=None):
        def typed_out(place, shape, dtype):
            if place in ("vmem", "hbm"):
                return spaces[place](shape, dtype)
            return jax.ShapeDtypeStruct(shape, dtype)

        def typed_in(place, value):
            if place in ("vmem", "hbm"):
                return pltpu.with_memory_space_constraint(value, spaces[place])
            return value

        limit = None if megabytes is None else megabytes << 20
        return pl.pallas_call(
            kernel,
            out_shape=tuple(typed_out(*out) for out in outs),
            in_specs=[pl.BlockSpec(memory_space=spaces[place]) for place, _ in ins],
            out_specs=tuple(pl.BlockSpec(memory_space=spaces[out[0]]) for out in outs),
            scratch_shapes=list(scratch),
            compiler_params=pltpu.CompilerParams(vmem_limit_bytes=limit),
        )(*(typed_in(*each_in) for each_in in ins))

    def peers_exchange(value):
        value = value.reshape(edge_size, per_peer, features)
        value = lax.all_to_all(value, "edge", split_axis=0, concat_axis=0, tiled=True)
        return value.reshape(slots_n, features)

    send_rows = sends.reshape(1, slots_n)
    slots_t, index_t, gains_t = edge_slot.T, rot_index.T, edge_gain.T
    table_t = jnp.transpose(rot_table, (1, 2, 0)).reshape(HARM * HARM, ROTS)
    wide = HARM * atoms_n
    outgoing, own = call(
        pick_kernel,
        [("vmem", (slots_n, features), BF16), ("vmem", (PACK_ROWS // node_size, C), BF16)],
        [("auto", value) for value in (send_rows, atoms, params.reshape(-1, C))],
    )
    slot_rows = peers_exchange(outgoing)
    by_distance = {0: own}
    for bit in reversed(range(node_bits)):
        for distance in list(by_distance):
            by_distance[distance | (1 << bit)] = swap(by_distance[distance], "node", bit)
    matrix_shapes = [(ZERO, ZERO), (ONE, ONE), (TWO, TWO)]
    unpacked_shapes = matrix_shapes * 2 + [(C, FFH)] * 2 + [(FFH, C)] * 3 + [(C, FFH)]
    atoms_t, cot_t, turn, gains_kept = call(
        arrange_kernel,
        [
            ("auto", (C, wide), BF16),
            ("auto", (C, wide), BF16),
            ("auto", (K * TURN_ROWS, atoms_n), F32),
            ("auto", (K, atoms_n), F32),
        ],
        [("smem", live_tiles)]
        + [("auto", value) for value in (atoms, cotangent, index_t, gains_t, table_t)],
    )
    unpacked = call(
        functools.partial(unpack_kernel, node_size),
        [("hbm", shape, BF16) for shape in unpacked_shapes],
        [("vmem", by_distance[distance]) for distance in range(node_size)],
        [
            *(pltpu.VMEM(shape, BF16) for shape in unpacked_shapes),
            pltpu.VMEM((PACK_ROWS, C), F32),
            pltpu.SemaphoreType.DMA((len(unpacked_shapes),)),
        ],
        megabytes=16,
    )
    sides = (slots_t, turn, gains_kept, *unpacked[3:], atoms_t, cot_t)
    read_again = (*unpacked[:3], turn, slots_t)
    output, height_grad, grad_mixed, keep, send = call(
        functools.partial(main_kernel, 4, node_size, atoms_n * node_size * edge_size),
        [
            ("hbm", (atoms_n, features), BF16),
            ("vmem", (C, wide), F32),
            ("vmem", (HARM, C, edges_n), BF16),
            ("vmem", (PACK_ROWS // 2, C), BF16),
            ("vmem", (PACK_ROWS // 2, C), BF16),
        ],
        [("vmem", slot_rows)]
        + [("hbm", value) for value in sides],
        [
            *(pltpu.VMEM(value.shape, value.dtype) for value in sides),
            pltpu.VMEM((atoms_n, features), BF16),
            pltpu.SemaphoreType.DMA((len(sides) + 1,)),
            pltpu.VMEM((HARM, C, edges_n), F32),
            pltpu.VMEM((HARM, C, edges_n), BF16),
            pltpu.VMEM((HARM, C, edges_n), F32),
            pltpu.VMEM((C, wide), F32),
            pltpu.VMEM((C, wide), BF16),
            pltpu.VMEM((FFH, wide), BF16),
            pltpu.VMEM((FFH, wide), BF16),
            pltpu.VMEM((PACK_ROWS, C), F32),
        ],
        megabytes=28,
    )
    slot_grad, height_rows = call(
        slot_kernel,
        [("vmem", (slots_n, features), F32), ("vmem", (atoms_n, features), F32)],
        [("vmem", grad_mixed), ("vmem", height_grad)]
        + [("hbm", value) for value in read_again],
        [
            *(pltpu.VMEM(value.shape, value.dtype) for value in read_again),
            pltpu.VMEM((HARM, C, edges_n), F32),
            pltpu.VMEM((HARM, C, edges_n), BF16),
            pltpu.VMEM((HARM, C, edges_n), BF16),
            pltpu.SemaphoreType.DMA((len(read_again),)),
        ],
        megabytes=20,
    )

    def add_low(left, right):
        return (left.astype(F32) + right.astype(F32)).astype(BF16)

    keep = add_low(keep, swap(send, "node", 0))
    quarter = keep.shape[0] // 4
    total = keep[:quarter].astype(F32)
    for number in (2, 3, 1):
        came = swap_edge(keep[number * quarter : (number + 1) * quarter], number)
        total = total + came.astype(F32)
    grads = total.astype(BF16)
    for bit in reversed(range(2, edge_bits)):
        grads = add_low(grads, swap(grads, "edge", bit))
    for bit in range(1, node_bits):
        half = grads.shape[0] // 2
        grads = add_low(grads[:half], swap(grads[half:], "node", bit))
    pieces = [grads]
    for number in (2, 3, 1):
        pieces.append(swap_edge(grads, number))
    first, third, fourth, second = pieces
    low = lax.axis_index("edge") & 1
    high = lax.axis_index("edge") & 2

    def exchange_if(flag, left, right):
        return jnp.where(flag, right, left), jnp.where(flag, left, right)

    first, second = exchange_if(low != 0, first, second)
    third, fourth = exchange_if(low != 0, third, fourth)
    first, third = exchange_if(high != 0, first, third)
    second, fourth = exchange_if(high != 0, second, fourth)
    grads = jnp.concatenate([first, second, third, fourth], axis=0).astype(F32)

    returned = peers_exchange(slot_grad)
    (grad_atoms,) = call(
        finish_kernel,
        [("auto", (atoms_n, features), BF16)],
        [("auto", send_rows), ("vmem", height_rows), ("vmem", returned)],
        megabytes=8,
    )

    def rows_of_lanes(value):
        return value.reshape(-1, C)

    new_params, new_one, new_two = adam_step(
        rows_of_lanes(params), rows_of_lanes(adam_m), rows_of_lanes(adam_v), grads
    )
    return (
        output,
        grad_atoms,
        new_params.reshape(-1),
        new_one.reshape(-1),
        new_two.reshape(-1),
    )


def solution(mesh):
    return jax.shard_map(
        shards,
        mesh=mesh,
        in_specs=(
            P(("node", "edge"), None),
            P(("node", "edge"), None),
            P("node"),
            P("node"),
            P("node"),
            P("node", "edge", None),
            P(("node", "edge"), None),
            P(("node", "edge"), None),
            P(),
            P(("node", "edge"), None),
            P("node", "edge"),
        ),
        out_specs=(
            P(("node", "edge"), None),
            P(("node", "edge"), None),
            P("node"),
            P("node"),
            P("node"),
        ),
        check_vma=False,
    )
```

```python
import functools

import jax
import jax.numpy as jnp
from jax import lax
from jax.experimental import pallas as pl
from jax.experimental.pallas import tpu as pltpu
from jax.sharding import PartitionSpec as P


C = 128
HARM = 9
FFH = 256
K = 4
TILE_ATOMS = 32
ROTS = 64
SUB = 8
TURN_ROWS = 88
GROUPS = 4
CHUNK = 4

harmonic_order = (0, 2, 6, 3, 7, 1, 5, 8, 4)
norm_epsilon = 1e-06
first_beta = 0.8
second_beta = 0.95
step_count = 100
learn_rate = 0.01
decay_rate = 0.01
adam_epsilon = 1e-08
grad_boost = 4.0

F32 = jnp.float32
BF16 = jnp.bfloat16

degree_block = (0, 1, 1, 1, 2, 2, 2, 2, 2)
entries = [
    (row, col, harmonic_order[row] * HARM + col)
    for row in range(HARM)
    for col in range(HARM)
    if degree_block[harmonic_order[row]] == degree_block[col]
]
cols_of = [[col for r, col, _ in entries if r == row] for row in range(HARM)]
rows_of = [[row for row, c, _ in entries if c == col] for col in range(HARM)]

ZERO, ONE, TWO = 3 * C, 4 * C, 2 * C
row_scale = [ZERO**-0.5] * 3 + [ONE**-0.5] * 4 + [TWO**-0.5] * 2
piece_rows = [9 * C, 4 * C, 4 * C, C, C, 2 * C, 2 * C, 2 * C]
piece_start = [sum(piece_rows[:i]) for i in range(len(piece_rows))]
PACK_ROWS = sum(piece_rows)


def lanes(number, width=C):
    return slice(number * width, (number + 1) * width)


def dot(left, right, left_dim=1, right_dim=0):
    return lax.dot_general(
        left, right, (((left_dim,), (right_dim,)), ((), ())), preferred_element_type=F32
    )


def split_parts(value, count):
    parts = []
    for _ in range(count):
        part = value.astype(BF16)
        parts.append(part)
        value = value - part.astype(F32)
    return parts


def as_low(mask):
    return jnp.where(mask, 1.0, 0.0).astype(BF16)


def pick_kernel(sends_ref, atoms_ref, params_ref, rows_ref, own_ref):
    shape = (atoms_ref.shape[0], sends_ref.shape[1])
    picks = as_low(lax.broadcasted_iota(jnp.int32, shape, 0) == sends_ref[...])
    rows_ref[...] = dot(picks, atoms_ref[...], 0, 0).astype(BF16)
    own_ref[...] = params_ref[...].astype(BF16)


def arrange_kernel(live_ref, atoms_ref, cot_ref, index_ref, gain_ref, table_ref, *outs):
    atoms_t_ref, cot_t_ref, turn_ref, gain_out_ref = outs
    atoms_n = atoms_ref.shape[0]
    is_live = lax.broadcasted_iota(jnp.int32, (K, atoms_n), 1) < live_ref[0, 0] * TILE_ATOMS
    gain_out_ref[...] = jnp.where(is_live, gain_ref[...], 0.0) * K**-0.5
    for col in range(HARM):
        atoms_t_ref[:, lanes(col, atoms_n)] = atoms_ref[:, lanes(col)].T
        cot_t_ref[:, lanes(col, atoms_n)] = cot_ref[:, lanes(col)].T
    pieces = split_parts(table_ref[...], 3)
    range_of_table = lax.broadcasted_iota(jnp.int32, (ROTS, atoms_n), 0)
    for k in range(K):
        chosen = as_low(range_of_table == index_ref[k : k + 1, :])
        turn_ref[pl.ds(k * TURN_ROWS, HARM * HARM), :] = sum(dot(piece, chosen) for piece in pieces)


def unpack_kernel(node_count, *refs):
    shard_refs = refs[:node_count]
    out_refs = refs[node_count : node_count + 12]
    built = refs[node_count + 12 : node_count + 24]
    packed, arrived = refs[node_count + 24 :]
    (
        zero_ref,
        one_ref,
        two_ref,
        zero_t_ref,
        one_t_ref,
        two_t_ref,
        gate_ref,
        up_ref,
        down_ref,
        gate_t_ref,
        up_t_ref,
        down_t_ref,
    ) = built
    copies = [
        pltpu.make_async_copy(source, target, arrived.at[number])
        for number, (source, target) in enumerate(zip(built, out_refs))
    ]
    node = lax.axis_index("node")

    shard_rows = PACK_ROWS // node_count
    for distance in range(node_count):
        first = pl.multiple_of((node ^ distance) * shard_rows, 8)
        packed[pl.ds(first, shard_rows), :] = shard_refs[distance][...].astype(F32)

    def unpack(piece, rows, width, *targets):
        for part in range(width):
            first = piece_start[piece] + part
            block = packed[pl.ds(first, rows, stride=width), :].astype(BF16)
            turned_block = block.T
            for target, turned, row, col, sign in targets:
                value = turned_block if turned else block
                value = value if sign > 0 else -value
                if turned:
                    target[col + part * C : col + (part + 1) * C, row : row + rows] = value
                else:
                    target[row : row + rows, col + part * C : col + (part + 1) * C] = value

    half = 2 * C
    unpack(0, ZERO, 3, (zero_t_ref, True, 0, 0, 1), (zero_ref, False, 0, 0, 1))
    copies[3].start()
    copies[0].start()
    for piece, matrix, turned, rows, places in (
        (1, one_ref, one_t_ref, half, (1, 4)),
        (3, two_ref, two_t_ref, C, (2, 5)),
    ):
        width = rows // C
        unpack(
            piece,
            rows,
            width,
            (turned, True, 0, 0, 1),
            (turned, True, rows, rows, 1),
            (matrix, False, 0, 0, 1),
            (matrix, False, rows, rows, 1),
        )
        unpack(
            piece + 1,
            rows,
            width,
            (turned, True, 0, rows, 1),
            (turned, True, rows, 0, -1),
            (matrix, False, 0, rows, 1),
            (matrix, False, rows, 0, -1),
        )
        for place in places:
            copies[place].start()
    unpack(5, C, 2, (gate_ref, False, 0, 0, 1), (gate_t_ref, True, 0, 0, 1))
    unpack(6, C, 2, (up_ref, False, 0, 0, 1), (up_t_ref, True, 0, 0, 1))
    unpack(7, FFH, 1, (down_ref, False, 0, 0, 1), (down_t_ref, True, 0, 0, 1))
    for copy in copies[6:]:
        copy.start()
    for copy in copies:
        copy.wait()


def turns_of(turn_ref, k, factors=None):
    values = {}
    for row, col, entry in entries:
        value = turn_ref[pl.ds(k * TURN_ROWS + entry, SUB, stride=0), :]
        values[row, col] = value if factors is None else value * factors[row]
    return values


def over_channels(body):
    def step(number, carry):
        for part in range(GROUPS):
            body(pl.multiple_of((number * GROUPS + part) * 2 * SUB, 2 * SUB))
        return carry

    lax.fori_loop(0, C // (2 * SUB * GROUPS), step, 0)


def flat(value):
    return value.reshape(value.shape[0] * value.shape[1], value.shape[2])


ZERO_PART, ONE_PART, TWO_PART = slice(0, 3), slice(3, 7), slice(7, 9)


def main_kernel(edge_parts, node_count, all_atoms, *refs):
    rows_ref = refs[0]
    sides = refs[1:15]
    output_ref, height_grad, grad_mixed, keep_ref, send_ref = refs[15:20]
    held = refs[20:34]
    slot_ref, turn, gain_ref = held[:3]
    (zero_t, one_t, two_t, gate_w, up_w, down_w, gate_t, up_t, down_t, atoms_t, cot_t) = held[3:]
    (
        output_rows,
        arrived,
        source,
        rotated,
        mixed,
        height,
        normed_low,
        hidden,
        grad_up,
        packed,
    ) = refs[34:]
    copies = [
        pltpu.make_async_copy(side, target, arrived.at[number])
        for number, (side, target) in enumerate(zip(sides, held))
    ]
    early, late = copies[:3], copies[3:]
    for copy in early + late:
        copy.start()
    output_copy = pltpu.make_async_copy(output_rows, output_ref, arrived.at[len(copies)])
    atoms_n = output_ref.shape[0]
    slots_n = rows_ref.shape[0]
    node = lax.axis_index("node")

    slot_range = lax.broadcasted_iota(jnp.int32, (slots_n, atoms_n), 0)
    for copy in early:
        copy.wait()
    taken = jnp.concatenate(
        [as_low(slot_range == slot_ref[k : k + 1, :]) for k in range(K)], axis=1
    )
    source[...] = dot(rows_ref[...], taken, 0, 0).reshape(source.shape)
    gains = gain_ref[...]

    for k in range(K):
        here = lanes(k, atoms_n)
        turns = turns_of(turn, k)

        def rotate(first, here=here, turns=turns):
            halves = []
            for start in (0, SUB):
                values = [source[col, pl.ds(first + start, SUB), here] for col in range(HARM)]
                halves.append(
                    [
                        sum(turns[row, col] * values[col] for col in cols_of[row])
                        for row in range(HARM)
                    ]
                )
            for row in range(HARM):
                pair = jnp.concatenate([halves[0][row], halves[1][row]], axis=0)
                rotated[row, pl.ds(first, 2 * SUB), here] = pair.astype(BF16)

        over_channels(rotate)
    for copy in late:
        copy.wait()
    for part, matrix in ((ZERO_PART, zero_t), (ONE_PART, one_t), (TWO_PART, two_t)):
        mixed[part] = dot(matrix[...], flat(rotated[part])).reshape(mixed[part].shape)

    for k in range(K):
        here = lanes(k, atoms_n)
        gain = jnp.broadcast_to(gains[k : k + 1, :], (SUB, atoms_n))
        turns = turns_of(turn, k, [gain * scale for scale in row_scale])

        def gather_messages(first, k=k, here=here, turns=turns):
            if k == 0:
                starts = [
                    atoms_t[pl.ds(first, 2 * SUB), lanes(col, atoms_n)].astype(F32)
                    for col in range(HARM)
                ]
            for start in (0, SUB):
                values = [mixed[row, pl.ds(first + start, SUB), here] for row in range(HARM)]
                target = pl.ds(first + start, SUB)
                for col in range(HARM):
                    there = lanes(col, atoms_n)
                    base = starts[col][start : start + SUB] if k == 0 else height[target, there]
                    total = sum(turns[row, col] * values[row] for row in rows_of[col])
                    height[target, there] = base + total

        over_channels(gather_messages)

    squares = jnp.zeros((C, atoms_n), F32)
    for col in range(HARM):
        value = height[:, lanes(col, atoms_n)]
        squares = squares + value * value
    mean = jnp.sum(squares, axis=0, keepdims=True) * (1.0 / (HARM * C))
    inverse = jnp.broadcast_to(lax.rsqrt(mean + norm_epsilon), (C, atoms_n))
    for col in range(HARM):
        here = lanes(col, atoms_n)
        normed_low[:, here] = (height[:, here] * inverse).astype(BF16)
    gate = jax.nn.sigmoid(dot(gate_t[...], normed_low[:, 0:atoms_n]) * C**-0.5)
    up_gate, down_gate = gate * C**-0.5, gate * FFH**-0.5
    chunks = [list(range(col, min(col + CHUNK, HARM))) for col in range(0, HARM, CHUNK)]
    gate_sum = jnp.zeros_like(gate)
    for chunk in chunks:
        wide = slice(chunk[0] * atoms_n, (chunk[-1] + 1) * atoms_n)
        up_here = dot(up_t[...], normed_low[:, wide])
        grad_here = dot(down_w[...], cot_t[:, wide])
        for place, col in enumerate(chunk):
            here, there = lanes(col, atoms_n), lanes(place, atoms_n)
            hidden[:, here] = (up_here[:, there] * up_gate).astype(BF16)
            grad_up[:, here] = (grad_here[:, there] * down_gate).astype(BF16)
            gate_sum = gate_sum + grad_here[:, there] * up_here[:, there]
    gate_sum = gate_sum * (C**-0.5 * FFH**-0.5)
    grad_gate = (gate_sum * gate * (1.0 - gate)).astype(BF16)
    overlap = jnp.zeros((C, atoms_n), F32)
    for chunk in chunks:
        wide = slice(chunk[0] * atoms_n, (chunk[-1] + 1) * atoms_n)
        projected = dot(down_t[...], hidden[:, wide])
        along = dot(up_w[...], grad_up[:, wide])
        for place, col in enumerate(chunk):
            here, there = lanes(col, atoms_n), lanes(place, atoms_n)
            value = height[:, here]
            output_rows[:, lanes(col)] = (
                (value + projected[:, there] * FFH**-0.5).astype(BF16).T
            )
            along_here = along[:, there]
            if col == 0:
                along_here = along_here + dot(gate_w[...], grad_gate)
            height_grad[:, here] = along_here
            overlap = overlap + along_here * value
    output_copy.start()
    overlap = jnp.sum(overlap, axis=0, keepdims=True) * (C**-0.5 / (HARM * C))
    scale = inverse * C**-0.5
    weight = inverse * inverse * (inverse * overlap)
    for col in range(HARM):
        here = lanes(col, atoms_n)
        height_grad[:, here] = (
            cot_t[:, here].astype(F32) + scale * height_grad[:, here] - weight * height[:, here]
        )

    for k in range(K):
        here = lanes(k, atoms_n)
        gain = jnp.broadcast_to(gains[k : k + 1, :], (SUB, atoms_n))
        turns = turns_of(turn, k, [gain] * HARM)

        def rotate_grads(first, here=here, turns=turns):
            halves = []
            for start in (0, SUB):
                target = pl.ds(first + start, SUB)
                values = [height_grad[target, lanes(col, atoms_n)] for col in range(HARM)]
                halves.append(
                    [
                        sum(turns[row, col] * values[col] for col in cols_of[row])
                        for row in range(HARM)
                    ]
                )
            for row in range(HARM):
                pair = jnp.concatenate([halves[0][row], halves[1][row]], axis=0)
                grad_mixed[row, pl.ds(first, 2 * SUB), here] = pair.astype(BF16)

        over_channels(rotate_grads)
    boost = grad_boost * all_atoms**-0.5

    def pack_piece(piece, rows, width, value):
        for part in range(width):
            packed[pl.ds(piece_start[piece] + part, rows, stride=width), :] = value[:, lanes(part)]

    def weight_grad(left, right, scale):
        return dot(left, right, 1, 1) * (scale * boost)

    zero_grad = weight_grad(flat(rotated[ZERO_PART]), flat(grad_mixed[ZERO_PART]), row_scale[0])
    pack_piece(0, ZERO, 3, zero_grad)
    one_grad = weight_grad(flat(rotated[ONE_PART]), flat(grad_mixed[ONE_PART]), row_scale[3])
    half = 2 * C
    pack_piece(1, half, 2, one_grad[:half, :half] + one_grad[half:, half:])
    pack_piece(2, half, 2, one_grad[:half, half:] - one_grad[half:, :half])
    two_grad = weight_grad(flat(rotated[TWO_PART]), flat(grad_mixed[TWO_PART]), row_scale[7])
    pack_piece(3, C, 1, two_grad[:C, :C] + two_grad[C:, C:])
    pack_piece(4, C, 1, two_grad[:C, C:] - two_grad[C:, :C])
    pack_piece(5, C, 2, weight_grad(normed_low[:, 0:atoms_n], grad_gate, C**-0.5))
    pack_piece(6, C, 2, weight_grad(normed_low[...], grad_up[...], C**-0.5))
    pack_piece(7, FFH, 1, weight_grad(hidden[...], cot_t[...], FFH**-0.5))
    shard_rows = PACK_ROWS // node_count
    part_rows = shard_rows // edge_parts
    edge_low = lax.axis_index("edge") & (edge_parts - 1)
    high_bits = node_count.bit_length() - 2
    blocks = []
    for low in range(2):
        for part in range(edge_parts):
            for place in range(node_count // 2):
                high = int(format(place, "b").zfill(high_bits)[::-1], 2) if high_bits else 0
                distance = low | (high << 1)
                blocks.append((node ^ distance) * shard_rows + (edge_low ^ part) * part_rows)
    half = len(blocks) // 2
    for number, first in enumerate(blocks):
        if part_rows % SUB == 0:
            first = pl.multiple_of(first, SUB)
        values = packed[pl.ds(first, part_rows), :].astype(BF16)
        target = keep_ref if number < half else send_ref
        target[lanes(number % half, part_rows), :] = values
    output_copy.wait()


def slot_kernel(grad_mixed, height_grad, *refs):
    sides, held = refs[:5], refs[7:12]
    slot_rows, height_rows_ref = refs[5:7]
    zero_w, one_w, two_w, turn, slot_ref = held
    mixed, source_high, source_low, arrived = refs[12:]
    copies = [
        pltpu.make_async_copy(side, target, arrived.at[number])
        for number, (side, target) in enumerate(zip(sides, held))
    ]
    for copy in copies:
        copy.start()
    slots_n = slot_rows.shape[0]
    atoms_n = slot_ref.shape[1]
    for col in range(HARM):
        height_rows_ref[:, lanes(col)] = height_grad[:, lanes(col, atoms_n)].T
    parts = ((ZERO_PART, zero_w), (ONE_PART, one_w), (TWO_PART, two_w))
    for (part, matrix), copy in zip(parts, copies):
        copy.wait()
        mixed[part] = dot(matrix[...], flat(grad_mixed[part])).reshape(mixed[part].shape)
    for copy in copies[3:]:
        copy.wait()
    for k in range(K):
        here = lanes(k, atoms_n)
        turns = turns_of(turn, k, row_scale)

        def rotate_back(first, here=here, turns=turns):
            halves = []
            for start in (0, SUB):
                values = [mixed[row, pl.ds(first + start, SUB), here] for row in range(HARM)]
                halves.append(
                    [
                        sum(turns[row, col] * values[row] for row in rows_of[col])
                        for col in range(HARM)
                    ]
                )
            for col in range(HARM):
                pair = jnp.concatenate([halves[0][col], halves[1][col]], axis=0)
                for target, part in zip((source_high, source_low), split_parts(pair, 2)):
                    target[col, pl.ds(first, 2 * SUB), here] = part

        over_channels(rotate_back)
    slot_range = lax.broadcasted_iota(jnp.int32, (slots_n, atoms_n), 0)
    taken = jnp.concatenate(
        [as_low(slot_range == slot_ref[k : k + 1, :]) for k in range(K)], axis=1
    )
    slot_rows[...] = dot(taken, flat(source_high[...]), 1, 1) + dot(
        taken, flat(source_low[...]), 1, 1
    )


def finish_kernel(sends_ref, height_rows_ref, back_ref, grad_ref):
    shape = (grad_ref.shape[0], sends_ref.shape[1])
    picks = as_low(lax.broadcasted_iota(jnp.int32, shape, 0) == sends_ref[...])
    for col in range(HARM):
        pieces = split_parts(back_ref[:, lanes(col)], 2)
        total = sum(dot(picks, piece) for piece in pieces)
        grad_ref[:, lanes(col)] = (height_rows_ref[:, lanes(col)] + total).astype(BF16)


def adam_step(params, moment_one, moment_two, gradient):
    new_one = first_beta * moment_one + (1.0 - first_beta) * gradient
    new_two = second_beta * moment_two + (1.0 - second_beta) * gradient * gradient
    corrected = (
        new_one
        / (1.0 - first_beta**step_count)
        / (jnp.sqrt(new_two / (1.0 - second_beta**step_count)) + adam_epsilon)
    )
    return (params - learn_rate * (corrected + decay_rate * params), new_one, new_two)


def swap(value, axis, bit):
    size = lax.axis_size(axis)
    return lax.ppermute(value, axis, [(i, i ^ (1 << bit)) for i in range(size)])


def swap_edge(value, step):
    return lax.ppermute(value, "edge", [(e, e ^ step) for e in range(lax.axis_size("edge"))])


def shards(
    atoms,
    cotangent,
    params,
    adam_m,
    adam_v,
    sends,
    edge_slot,
    rot_index,
    rot_table,
    edge_gain,
    live_tiles,
):
    node_size = lax.axis_size("node")
    edge_size = lax.axis_size("edge")
    node_bits = node_size.bit_length() - 1
    edge_bits = edge_size.bit_length() - 1
    atoms_n, features = atoms.shape
    slots_n = sends.shape[-1]
    per_peer = slots_n // edge_size
    edges_n = atoms_n * K

    spaces = {"vmem": pltpu.VMEM, "smem": pltpu.SMEM, "hbm": pltpu.HBM, "auto": pltpu.VMEM}

    def call(kernel, outs, ins, scratch=(), megabytes=None):
        def typed_out(place, shape, dtype):
            if place in ("vmem", "hbm"):
                return spaces[place](shape, dtype)
            return jax.ShapeDtypeStruct(shape, dtype)

        def typed_in(place, value):
            if place in ("vmem", "hbm"):
                return pltpu.with_memory_space_constraint(value, spaces[place])
            return value

        limit = None if megabytes is None else megabytes << 20
        return pl.pallas_call(
            kernel,
            out_shape=tuple(typed_out(*out) for out in outs),
            in_specs=[pl.BlockSpec(memory_space=spaces[place]) for place, _ in ins],
            out_specs=tuple(pl.BlockSpec(memory_space=spaces[out[0]]) for out in outs),
            scratch_shapes=list(scratch),
            compiler_params=pltpu.CompilerParams(vmem_limit_bytes=limit),
        )(*(typed_in(*each_in) for each_in in ins))

    def peers_exchange(value):
        value = value.reshape(edge_size, per_peer, features)
        value = lax.all_to_all(value, "edge", split_axis=0, concat_axis=0, tiled=True)
        return value.reshape(slots_n, features)

    send_rows = sends.reshape(1, slots_n)
    slots_t, index_t, gains_t = edge_slot.T, rot_index.T, edge_gain.T
    table_t = jnp.transpose(rot_table, (1, 2, 0)).reshape(HARM * HARM, ROTS)
    wide = HARM * atoms_n
    outgoing, own = call(
        pick_kernel,
        [("vmem", (slots_n, features), BF16), ("vmem", (PACK_ROWS // node_size, C), BF16)],
        [("auto", value) for value in (send_rows, atoms, params.reshape(-1, C))],
    )
    slot_rows = peers_exchange(outgoing)
    by_distance = {0: own}
    for bit in reversed(range(node_bits)):
        for distance in list(by_distance):
            by_distance[distance | (1 << bit)] = swap(by_distance[distance], "node", bit)
    matrix_shapes = [(ZERO, ZERO), (ONE, ONE), (TWO, TWO)]
    unpacked_shapes = matrix_shapes * 2 + [(C, FFH)] * 2 + [(FFH, C)] * 3 + [(C, FFH)]
    atoms_t, cot_t, turn, gains_kept = call(
        arrange_kernel,
        [
            ("auto", (C, wide), BF16),
            ("auto", (C, wide), BF16),
            ("auto", (K * TURN_ROWS, atoms_n), F32),
            ("auto", (K, atoms_n), F32),
        ],
        [("smem", live_tiles)]
        + [("auto", value) for value in (atoms, cotangent, index_t, gains_t, table_t)],
    )
    unpacked = call(
        functools.partial(unpack_kernel, node_size),
        [("hbm", shape, BF16) for shape in unpacked_shapes],
        [("vmem", by_distance[distance]) for distance in range(node_size)],
        [
            *(pltpu.VMEM(shape, BF16) for shape in unpacked_shapes),
            pltpu.VMEM((PACK_ROWS, C), F32),
            pltpu.SemaphoreType.DMA((len(unpacked_shapes),)),
        ],
        megabytes=16,
    )
    sides = (slots_t, turn, gains_kept, *unpacked[3:], atoms_t, cot_t)
    read_again = (*unpacked[:3], turn, slots_t)
    output, height_grad, grad_mixed, keep, send = call(
        functools.partial(main_kernel, 4, node_size, atoms_n * node_size * edge_size),
        [
            ("hbm", (atoms_n, features), BF16),
            ("vmem", (C, wide), F32),
            ("vmem", (HARM, C, edges_n), BF16),
            ("vmem", (PACK_ROWS // 2, C), BF16),
            ("vmem", (PACK_ROWS // 2, C), BF16),
        ],
        [("vmem", slot_rows)]
        + [("hbm", value) for value in sides],
        [
            *(pltpu.VMEM(value.shape, value.dtype) for value in sides),
            pltpu.VMEM((atoms_n, features), BF16),
            pltpu.SemaphoreType.DMA((len(sides) + 1,)),
            pltpu.VMEM((HARM, C, edges_n), F32),
            pltpu.VMEM((HARM, C, edges_n), BF16),
            pltpu.VMEM((HARM, C, edges_n), F32),
            pltpu.VMEM((C, wide), F32),
            pltpu.VMEM((C, wide), BF16),
            pltpu.VMEM((FFH, wide), BF16),
            pltpu.VMEM((FFH, wide), BF16),
            pltpu.VMEM((PACK_ROWS, C), F32),
        ],
        megabytes=28,
    )
    slot_grad, height_rows = call(
        slot_kernel,
        [("vmem", (slots_n, features), F32), ("vmem", (atoms_n, features), F32)],
        [("vmem", grad_mixed), ("vmem", height_grad)]
        + [("hbm", value) for value in read_again],
        [
            *(pltpu.VMEM(value.shape, value.dtype) for value in read_again),
            pltpu.VMEM((HARM, C, edges_n), F32),
            pltpu.VMEM((HARM, C, edges_n), BF16),
            pltpu.VMEM((HARM, C, edges_n), BF16),
            pltpu.SemaphoreType.DMA((len(read_again),)),
        ],
        megabytes=20,
    )

    def add_low(left, right):
        return (left.astype(F32) + right.astype(F32)).astype(BF16)

    keep = add_low(keep, swap(send, "node", 0))
    quarter = keep.shape[0] // 4
    total = keep[:quarter].astype(F32)
    for number in (2, 3, 1):
        came = swap_edge(keep[number * quarter : (number + 1) * quarter], number)
        total = total + came.astype(F32)
    grads = total.astype(BF16)
    for bit in reversed(range(2, edge_bits)):
        grads = add_low(grads, swap(grads, "edge", bit))
    for bit in range(1, node_bits):
        half = grads.shape[0] // 2
        grads = add_low(grads[:half], swap(grads[half:], "node", bit))
    pieces = [grads]
    for number in (2, 3, 1):
        pieces.append(swap_edge(grads, number))
    first, third, fourth, second = pieces
    low = lax.axis_index("edge") & 1
    high = lax.axis_index("edge") & 2

    def exchange_if(flag, left, right):
        return jnp.where(flag, right, left), jnp.where(flag, left, right)

    first, second = exchange_if(low != 0, first, second)
    third, fourth = exchange_if(low != 0, third, fourth)
    first, third = exchange_if(high != 0, first, third)
    second, fourth = exchange_if(high != 0, second, fourth)
    grads = jnp.concatenate([first, second, third, fourth], axis=0).astype(F32)

    returned = peers_exchange(slot_grad)
    (grad_atoms,) = call(
        finish_kernel,
        [("auto", (atoms_n, features), BF16)],
        [("auto", send_rows), ("vmem", height_rows), ("vmem", returned)],
        megabytes=8,
    )

    def rows_of_lanes(value):
        return value.reshape(-1, C)

    new_params, new_one, new_two = adam_step(
        rows_of_lanes(params), rows_of_lanes(adam_m), rows_of_lanes(adam_v), grads
    )
    return (
        output,
        grad_atoms,
        new_params.reshape(-1),
        new_one.reshape(-1),
        new_two.reshape(-1),
    )


def solution(mesh):
    return jax.shard_map(
        shards,
        mesh=mesh,
        in_specs=(
            P(("node", "edge"), None),
            P(("node", "edge"), None),
            P("node"),
            P("node"),
            P("node"),
            P("node", "edge", None),
            P(("node", "edge"), None),
            P(("node", "edge"), None),
            P(),
            P(("node", "edge"), None),
            P("node", "edge"),
        ),
        out_specs=(
            P(("node", "edge"), None),
            P(("node", "edge"), None),
            P("node"),
            P("node"),
            P("node"),
        ),
        check_vma=False,
    )
```
